32 devices in a mesh: dp: 4 (over z), ctx: 8 (over y, x, core).
Axes of the slice: x: 2, y: 2, z: 4, core: 2. Of those that a mesh axis runs over, the one named last changes fastest.
Arguments:
- block_input: bfloat16 [2, 4, 1024, 768], P(None, 'dp', 'ctx'), may hold values from -6 to 6
- out_grad: bfloat16 [2, 4, 1024, 768], P(None, 'dp', 'ctx'), may hold values from -6 to 6
- prefix_len: int32 [2, 4], P(None, 'dp'), may hold values from 102 to 512
- attn_gain: bfloat16 [768], P(('dp', 'ctx')), may hold values from 0.5 to 1.5
- q_weight: bfloat16 [768, 768], P(('dp', 'ctx')), may hold values from -0.21875 to 0.21875
- k_weight: bfloat16 [768, 768], P(('dp', 'ctx')), may hold values from -0.21875 to 0.21875
- v_weight: bfloat16 [768, 768], P(('dp', 'ctx')), may hold values from -0.21875 to 0.21875
- conv_q: bfloat16 [3, 768], P(None, ('dp', 'ctx')), may hold values from -2.5 to 2.5
- conv_k: bfloat16 [3, 768], P(None, ('dp', 'ctx')), may hold values from -2.5 to 2.5
- conv_v: bfloat16 [3, 768], P(None, ('dp', 'ctx')), may hold values from -2.5 to 2.5
- out_weight: bfloat16 [768, 768], P(('dp', 'ctx')), may hold values from -3 to 3
- out_bias: bfloat16 [768], P(('dp', 'ctx')), may hold values from -1.75 to 1.75
- ffn_gain: bfloat16 [768], P(('dp', 'ctx')), may hold values from 0.5 to 1.5
- up_weight: bfloat16 [768, 3072], P(('dp', 'ctx')), may hold values from -0.21875 to 0.21875
- up_bias: bfloat16 [3072], P(('dp', 'ctx')), may hold values from -3 to 3
- down_weight: bfloat16 [3072, 768], P(('dp', 'ctx')), may hold values from -0.109375 to 0.109375
- down_bias: bfloat16 [768], P(('dp', 'ctx')), may hold values from -1.75 to 1.75
Outputs:
- block_output: bfloat16 [2, 4, 1024, 768], P(None, 'dp', 'ctx')
- input_grad: float32 [2, 4, 1024, 768], P(None, 'dp', 'ctx')
- attn_gain_grad: float32 [768], P(('dp', 'ctx'))
- q_weight_grad: float32 [768, 768], P(('dp', 'ctx'))
- k_weight_grad: float32 [768, 768], P(('dp', 'ctx'))
- v_weight_grad: float32 [768, 768], P(('dp', 'ctx'))
- conv_q_grad: float32 [3, 768], P(None, ('dp', 'ctx'))
- conv_k_grad: float32 [3, 768], P(None, ('dp', 'ctx'))
- conv_v_grad: float32 [3, 768], P(None, ('dp', 'ctx'))
- out_weight_grad: float32 [768, 768], P(('dp', 'ctx'))
- out_bias_grad: float32 [768], P(('dp', 'ctx'))
- ffn_gain_grad: float32 [768], P(('dp', 'ctx'))
- up_weight_grad: float32 [768, 3072], P(('dp', 'ctx'))
- up_bias_grad: float32 [3072], P(('dp', 'ctx'))
- down_weight_grad: float32 [3072, 768], P(('dp', 'ctx'))
- down_bias_grad: float32 [768], P(('dp', 'ctx'))
The draws below stay inside these ranges and needn't reach their ends.
All inputs are finite; a program needn't handle non-finite values.
Results may differ from the reference program's by a relative error of at most 0.019.
Values may be sent and summed in bfloat16 or wider, within the bound.
No kernel may reach another device: no remote copies, remote signals or barrier semaphores. Data moves between devices by JAX's collectives and lax.ppermute only.
A program may use at most 192 MiB of HBM per device.

```python
import jax
import jax.numpy as jnp
from jax import lax

D = 768
HEADS = 12
HEAD = 64
FF = 3072
MB = 2
SEQ_LEN = 1024
SEQS = 4


def place_ends(values, stream_key, smallest, top_value):
    longest = values.shape.index(max(values.shape))
    spots = []
    for shift in (0, 1):
        where = [jax.random.randint(jax.random.fold_in(stream_key, axis), (), 0, length) for axis, length in enumerate(values.shape)]
        where[longest] = (where[longest] + shift) % values.shape[longest]
        spots.append(tuple(where))
    return values.at[spots[0]].set(smallest).at[spots[1]].set(top_value)


def steps_of(rng, shape, cuts, least, top_value):
    loudness, own = 1.0, jax.random.fold_in(rng, 6)
    for position, parts in cuts:
        draws = jnp.exp(jax.random.uniform(jax.random.fold_in(own, position), (parts,), jnp.float32, least / len(cuts), top_value / len(cuts)))
        loudness = loudness * jnp.repeat(draws, shape[position] // parts).reshape([-1 if axis == position else 1 for axis in range(len(shape))])
    return loudness


def centred(own_key, dims, deviation, bound, split=(), dtype=jnp.bfloat16):
    loudness = steps_of(own_key, dims, split, -0.22, 0.18) if split else 1.0
    array = jax.random.normal(own_key, dims, jnp.float32) * deviation * loudness
    return jnp.minimum(jnp.maximum(array, -bound), bound).astype(dtype)


def setup_inputs(seed: int = 0) -> dict:
    streams_of = jax.random.split(jax.random.key(seed), 18)
    return {
        "block_input": centred(streams_of[0], (MB, SEQS, SEQ_LEN, D), 1.0, 6.0, ((1, 4), (2, 8))),
        "out_grad": centred(streams_of[1], (MB, SEQS, SEQ_LEN, D), 1.0, 6.0, ((1, 4), (2, 8))),
        "prefix_len": place_ends(jax.random.randint(streams_of[2], (MB, SEQS), SEQ_LEN // 10, SEQ_LEN // 2 + 1), jax.random.fold_in(streams_of[2], 1), SEQ_LEN // 10, (SEQ_LEN // 2 + 1) - 1).astype(jnp.int32),
        "attn_gain": jnp.clip(1.0 + 0.1 * jax.random.normal(streams_of[3], (D,), jnp.float32), 0.5, 1.5).astype(jnp.bfloat16),
        "q_weight": centred(streams_of[4], (D, D), D ** -0.5, 0.21875, ((0, 32),)),
        "k_weight": centred(streams_of[5], (D, D), D ** -0.5, 0.21875, ((0, 32),)),
        "v_weight": centred(streams_of[6], (D, D), D ** -0.5, 0.21875, ((0, 32),)),
        "conv_q": centred(streams_of[7], (3, D), 0.6, 2.5, ((1, 32),)),
        "conv_k": centred(streams_of[8], (3, D), 0.6, 2.5, ((1, 32),)),
        "conv_v": centred(streams_of[9], (3, D), 0.6, 2.5, ((1, 32),)),
        "out_weight": centred(streams_of[10], (D, D), 4 ** -0.5, 3.0, ((0, 32),)),
        "out_bias": centred(streams_of[11], (D,), 0.3, 1.75, ((0, 32),)),
        "ffn_gain": jnp.clip(1.0 + 0.1 * jax.random.normal(streams_of[12], (D,), jnp.float32), 0.5, 1.5).astype(jnp.bfloat16),
        "up_weight": centred(streams_of[13], (D, FF), D ** -0.5, 0.21875, ((0, 32),)),
        "up_bias": centred(streams_of[14], (FF,), 0.5, 3.0, ((0, 32),)),
        "down_weight": centred(streams_of[15], (FF, D), FF ** -0.5, 0.109375, ((0, 32),)),
        "down_bias": centred(streams_of[16], (D,), 0.3, 1.75, ((0, 32),)),
    }


EPS = 1e-06
NEG = -1e+30
HIGH = lax.Precision.HIGHEST

@jax.custom_vjp
def low(v):
    return lax.optimization_barrier(v.astype(jnp.bfloat16)).astype(jnp.float32)

@jax.custom_vjp
def low_back(v):
    return v

def low_keep(v):
    return (low(v), None)

def low_pass(kept, grad):
    return (grad,)

def back_keep(v):
    return (v, None)

def back_low(kept, grad):
    return (low(grad),)
low.defvjp(low_keep, low_pass)
low_back.defvjp(back_keep, back_low)

def matmul(left, right):
    return jnp.dot(left, right, precision=HIGH, preferred_element_type=jnp.float32)

def rms_norm(values, gain_vec):
    return values * lax.rsqrt(lax.optimization_barrier(jnp.mean(values * values, axis=-1, keepdims=True)) + EPS) * gain_vec

def causal_conv(values, kernel):
    one_back = jnp.pad(values, ((1, 0), (0, 0)))[:-1]
    two_back = jnp.pad(values, ((2, 0), (0, 0)))[:-2]
    return kernel[0] * values + kernel[1] * one_back + kernel[2] * two_back

def attend(query, key_rows, value_rows, prefix):
    length = query.shape[0]
    block_rows = min(512, length)
    score_scale = HEAD ** (-0.5)
    heads_q = query.reshape(length, HEADS, HEAD)
    heads_k = key_rows.reshape(length, HEADS, HEAD)
    heads_v = value_rows.reshape(length, HEADS, HEAD)
    columns = jnp.arange(length).astype(jnp.int32)

    def one_block(row_start):
        row_ids = row_start + jnp.arange(block_rows).astype(jnp.int32)
        q_block = lax.dynamic_slice_in_dim(heads_q, row_start, block_rows, 0)
        raw_scores = low_back(jnp.einsum('qhe,khe->hqk', q_block, heads_k, precision=HIGH))
        allowed = (columns[None, :] <= row_ids[:, None]) | (columns[None, :] < prefix)
        scores = jnp.where(allowed[None], raw_scores * score_scale, NEG)
        row_top = lax.optimization_barrier(jnp.max(scores, axis=-1, keepdims=True))
        expo_vals = jnp.exp(scores - row_top)
        probs = low(expo_vals / lax.optimization_barrier(jnp.sum(expo_vals, axis=-1, keepdims=True)))
        return jnp.einsum('hqk,khe->qhe', probs, heads_v, precision=HIGH)
    row_starts = (jnp.arange(length // block_rows) * block_rows).astype(jnp.int32)
    outcome = lax.map(jax.checkpoint(one_block), row_starts)
    return outcome.reshape(length, HEADS * HEAD)

def layer(inputs, prefix, attn_gain, q_weight, k_weight, v_weight, conv_q, conv_k, conv_v, out_weight, out_bias, ffn_gain, up_weight, up_bias, down_weight, down_bias):
    normed = low(rms_norm(inputs, attn_gain))
    q_lin = low_back(matmul(normed, q_weight))
    k_lin = low_back(matmul(normed, k_weight))
    v_lin = low_back(matmul(normed, v_weight))
    query = low(causal_conv(q_lin, conv_q))
    key_rows = low(causal_conv(k_lin, conv_k))
    value_rows = low(causal_conv(v_lin, conv_v))
    attended = low_back(low(attend(query, key_rows, value_rows, prefix)))
    branch = low_back(matmul(attended, out_weight) + out_bias)
    resid = inputs + branch
    normed_ffn = low(rms_norm(resid, ffn_gain))
    pre_act = low_back(matmul(normed_ffn, up_weight) + up_bias)
    hidden = low_back(low(jnp.square(jax.nn.relu(pre_act))))
    return resid + matmul(hidden, down_weight) + down_bias

def reference(block_input, out_grad, prefix_len, attn_gain, q_weight, k_weight, v_weight, conv_q, conv_k, conv_v, out_weight, out_bias, ffn_gain, up_weight, up_bias, down_weight, down_bias):
    params = tuple((item.astype(jnp.float32) for item in (attn_gain, q_weight, k_weight, v_weight, conv_q, conv_k, conv_v, out_weight, out_bias, ffn_gain, up_weight, up_bias, down_weight, down_bias)))
    length = block_input.shape[2]
    features = block_input.shape[3]
    inputs = block_input.astype(jnp.float32).reshape(-1, length, features)
    cotangents = out_grad.astype(jnp.float32).reshape(-1, length, features)
    prefixes = prefix_len.reshape(-1).astype(jnp.int32)

    def step_one(carry, item):
        seq_in, seq_cot, seq_prefix = item

        def forward(values, *weights):
            return layer(values, seq_prefix, *weights)
        result, pull = jax.vjp(forward, seq_in, *params)
        grads = pull(seq_cot)
        return (tuple((earlier + later for earlier, later in zip(carry, grads[1:]))), (result.astype(jnp.bfloat16), grads[0]))
    zeros_init = tuple((jnp.zeros(item.shape, jnp.float32) for item in params))
    totals, (results, input_grads) = lax.scan(step_one, zeros_init, (inputs, cotangents, prefixes))
    shape_all = block_input.shape
    return (results.reshape(shape_all), input_grads.reshape(shape_all), totals[0], totals[1], totals[2], totals[3], totals[4], totals[5], totals[6], totals[7], totals[8], totals[9], totals[10], totals[11], totals[12], totals[13])
```

```python
import functools

import jax
import jax.numpy as jnp
from jax import lax
from jax.experimental import pallas as pl
from jax.experimental.pallas import tpu as pltpu
from jax.sharding import PartitionSpec as P

HEADS = 12
HEAD = 64


EPS = 1e-06
NEG = -1e30


def shifted(shard, axis, by):
    peers = lax.axis_size(axis)
    pairs = [(i, i + by) for i in range(peers) if 0 <= i + by < peers]
    return lax.ppermute(shard, axis, pairs)


def norm_rows(values, gain_vec):
    factor = lax.rsqrt(jnp.mean(values * values, axis=-1, keepdims=True) + EPS)
    return (factor, values * factor * gain_vec)


def norm_back(values, factor, gain_vec, grad_out):
    weighted = grad_out * gain_vec
    inner = jnp.mean(weighted * values, axis=-1, keepdims=True)
    return (
        factor * weighted - values * factor**3 * inner,
        jnp.sum(grad_out * values * factor, axis=0),
    )


def outer_sum(left, right):
    return lax.dot_general(
        left, right, (((0,), (0,)), ((), ())), preferred_element_type=jnp.float32
    )


def back_prod(grad_rows, weight):
    return lax.dot_general(
        grad_rows, weight, (((1,), (1,)), ((), ())), preferred_element_type=jnp.float32
    )


def scores_of(query, key_part, key_start, offset, prefix):
    raw_scores = jnp.einsum("sthe,skhe->shtk", query, key_part, preferred_element_type=jnp.float32)
    row_ids = offset + jnp.arange(query.shape[1], dtype=jnp.int32)
    col_ids = key_start + jnp.arange(key_part.shape[1], dtype=jnp.int32)
    allowed = (col_ids[None, None, :] <= row_ids[None, :, None]) | (
        col_ids[None, None, :] < prefix[:, None, None]
    )
    return jnp.where(allowed[:, None], raw_scores * HEAD ** (-0.5), NEG)


def forward_pass(inputs, prefix, weights, offset):
    (
        gain_attn,
        w_query,
        w_key,
        w_value,
        conv_query,
        conv_key,
        conv_value,
        w_out,
        b_out,
        gain_ffn,
        w_up,
        b_up,
        w_down,
        b_down,
    ) = weights
    seq_count, tok_len, features = inputs.shape
    length = tok_len * lax.axis_size("ctx")
    key_block = min(512, length)
    block_count = length // key_block
    rows_in = inputs.reshape(seq_count * tok_len, features)
    factor_attn, normed = norm_rows(rows_in, gain_attn.astype(jnp.float32))
    normed_low = normed.astype(jnp.bfloat16)
    w_joint = jnp.concatenate([w_query, w_key, w_value], axis=1)
    kernel = jnp.concatenate([conv_query, conv_key, conv_value], axis=1).astype(jnp.float32)
    linear = jnp.dot(normed_low, w_joint, preferred_element_type=jnp.float32).reshape(
        seq_count, tok_len, 3 * features
    )
    before = shifted(linear[:, tok_len - 2 :], "ctx", 1)
    padded = jnp.concatenate([before, linear], axis=1)
    mixed = (
        kernel[0] * padded[:, 2:]
        + kernel[1] * padded[:, 1 : tok_len + 1]
        + kernel[2] * padded[:, :tok_len]
    ).astype(jnp.bfloat16)
    query = mixed[:, :, :features].reshape(seq_count, tok_len, HEADS, HEAD)
    keys_all, values_all = (
        lax.all_gather(mixed[:, :, features : 2 * features], "ctx", axis=1, tiled=True),
        lax.all_gather(mixed[:, :, 2 * features :], "ctx", axis=1, tiled=True),
    )
    keys_all = keys_all.reshape(seq_count, length, HEADS, HEAD)
    values_all = values_all.reshape(seq_count, length, HEADS, HEAD)
    block_ids = jnp.arange(block_count, dtype=jnp.int32)

    def max_turn(carry, key_index):
        row_top, row_total = carry
        key_start = key_index * key_block
        key_part = lax.dynamic_slice_in_dim(keys_all, key_start, key_block, 1)
        scores = scores_of(query, key_part, key_start, offset, prefix)
        new_top = jnp.maximum(row_top, jnp.max(scores, axis=-1))
        row_total = row_total * jnp.exp(row_top - new_top) + jnp.sum(
            jnp.exp(scores - new_top[..., None]), axis=-1
        )
        return ((new_top, row_total), None)

    stat_shape = (seq_count, HEADS, tok_len)
    (row_top, row_total), unused = lax.scan(
        max_turn,
        (jnp.full(stat_shape, NEG, jnp.float32), jnp.zeros(stat_shape, jnp.float32)),
        block_ids,
    )
    log_total = row_top + jnp.log(row_total)

    def out_turn(summed, key_index):
        key_start = key_index * key_block
        key_part = lax.dynamic_slice_in_dim(keys_all, key_start, key_block, 1)
        value_part = lax.dynamic_slice_in_dim(values_all, key_start, key_block, 1)
        scores = scores_of(query, key_part, key_start, offset, prefix)
        probs = jnp.exp(scores - log_total[..., None]).astype(jnp.bfloat16)
        return (
            summed
            + jnp.einsum("shtk,skhe->sthe", probs, value_part, preferred_element_type=jnp.float32),
            None,
        )

    attended, unused = lax.scan(out_turn, jnp.zeros(query.shape, jnp.float32), block_ids)
    attn_low = attended.astype(jnp.bfloat16).reshape(seq_count * tok_len, features)
    resid = rows_in + (
        jnp.dot(attn_low, w_out, preferred_element_type=jnp.float32) + b_out.astype(jnp.float32)
    )
    factor_ffn, normed2 = norm_rows(resid, gain_ffn.astype(jnp.float32))
    normed_ffn = normed2.astype(jnp.bfloat16)
    pre_act = jnp.dot(normed_ffn, w_up, preferred_element_type=jnp.float32) + b_up.astype(
        jnp.float32
    )
    hidden_low = jnp.square(jax.nn.relu(pre_act)).astype(jnp.bfloat16)
    result = (
        resid
        + jnp.dot(hidden_low, w_down, preferred_element_type=jnp.float32)
        + b_down.astype(jnp.float32)
    )
    saved = (
        rows_in,
        factor_attn,
        normed_low,
        padded,
        query,
        keys_all,
        values_all,
        log_total,
        attended,
        attn_low,
        resid,
        factor_ffn,
        normed_ffn,
        pre_act,
        hidden_low,
    )
    return (saved, result)


def backward_pass(saved, cot_low, prefix, weights, offset):
    (
        rows_in,
        factor_attn,
        normed_low,
        padded,
        query,
        keys_all,
        values_all,
        log_total,
        attended,
        attn_low,
        resid,
        factor_ffn,
        normed_ffn,
        pre_act,
        hidden_low,
    ) = saved
    (
        gain_attn,
        w_query,
        w_key,
        w_value,
        conv_query,
        conv_key,
        conv_value,
        w_out,
        b_out,
        gain_ffn,
        w_up,
        b_up,
        w_down,
        b_down,
    ) = weights
    seq_count, tok_len = (query.shape[0], query.shape[1])
    features = rows_in.shape[1]
    length = keys_all.shape[1]
    key_block = min(512, length)
    block_count = length // key_block
    cot_rows = cot_low.reshape(seq_count * tok_len, features)
    cot_full = cot_rows.astype(jnp.float32)
    grad_bdown = jnp.sum(cot_full, axis=0)
    grad_wdown = outer_sum(hidden_low, cot_rows)
    grad_hidden = back_prod(cot_rows, w_down).astype(jnp.bfloat16)
    grad_pre = (grad_hidden.astype(jnp.float32) * 2.0 * jax.nn.relu(pre_act)).astype(jnp.bfloat16)
    grad_bup = jnp.sum(grad_pre.astype(jnp.float32), axis=0)
    grad_wup = outer_sum(normed_ffn, grad_pre)
    grad_normed = back_prod(grad_pre, w_up)
    resid_part, grad_gffn = norm_back(resid, factor_ffn, gain_ffn.astype(jnp.float32), grad_normed)
    grad_resid = cot_full + resid_part
    grad_branch = grad_resid.astype(jnp.bfloat16)
    grad_bout = jnp.sum(grad_branch.astype(jnp.float32), axis=0)
    grad_wout = outer_sum(attn_low, grad_branch)
    grad_attn = (
        back_prod(grad_branch, w_out).astype(jnp.bfloat16).reshape(seq_count, tok_len, HEADS, HEAD)
    )
    delta = jnp.einsum("sthe,sthe->sht", grad_attn.astype(jnp.float32), attended)
    block_ids = jnp.arange(block_count, dtype=jnp.int32)

    def grad_terms(key_index):
        key_start = key_index * key_block
        key_part = lax.dynamic_slice_in_dim(keys_all, key_start, key_block, 1)
        value_part = lax.dynamic_slice_in_dim(values_all, key_start, key_block, 1)
        scores = scores_of(query, key_part, key_start, offset, prefix)
        probs = jnp.exp(scores - log_total[..., None])
        grad_probs = jnp.einsum(
            "sthe,skhe->shtk", grad_attn, value_part, preferred_element_type=jnp.float32
        )
        grad_scores = (probs * (grad_probs - delta[..., None]) * HEAD ** (-0.5)).astype(
            jnp.bfloat16
        )
        return (key_part, probs, grad_scores)

    def back_turn(summed, key_index):
        key_part, probs, grad_scores = grad_terms(key_index)
        summed = summed + jnp.einsum(
            "shtk,skhe->sthe", grad_scores, key_part, preferred_element_type=jnp.float32
        )
        grad_keys = jnp.einsum(
            "shtk,sthe->skhe", grad_scores, query, preferred_element_type=jnp.float32
        )
        grad_values = jnp.einsum(
            "shtk,sthe->skhe",
            probs.astype(jnp.bfloat16),
            grad_attn,
            preferred_element_type=jnp.float32,
        )
        return (summed, (grad_keys, grad_values))

    grad_query, (grad_keys, grad_values) = lax.scan(
        back_turn, jnp.zeros(query.shape, jnp.float32), block_ids
    )
    grad_keys = jnp.moveaxis(grad_keys, 0, 1).reshape(seq_count, length, features)
    grad_values = jnp.moveaxis(grad_values, 0, 1).reshape(seq_count, length, features)
    own_keys, own_values = (
        lax.psum_scatter(
            grad_keys.astype(jnp.bfloat16), "ctx", scatter_dimension=1, tiled=True
        ).astype(jnp.float32),
        lax.psum_scatter(
            grad_values.astype(jnp.bfloat16), "ctx", scatter_dimension=1, tiled=True
        ).astype(jnp.float32),
    )
    grad_mixed = jnp.concatenate(
        [grad_query.reshape(seq_count, tok_len, features), own_keys, own_values], axis=2
    )
    after = shifted(grad_mixed[:, :2], "ctx", -1)
    extended = jnp.concatenate([grad_mixed, after], axis=1)
    kernel = jnp.concatenate([conv_query, conv_key, conv_value], axis=1).astype(jnp.float32)
    grad_linear = (
        kernel[0] * extended[:, :tok_len]
        + kernel[1] * extended[:, 1 : tok_len + 1]
        + kernel[2] * extended[:, 2:]
    ).astype(jnp.bfloat16)
    grad_kernel = jnp.stack(
        [
            jnp.sum(grad_mixed * padded[:, 2:], axis=(0, 1)),
            jnp.sum(grad_mixed * padded[:, 1 : tok_len + 1], axis=(0, 1)),
            jnp.sum(grad_mixed * padded[:, :tok_len], axis=(0, 1)),
        ]
    )
    grad_lin_rows = grad_linear.reshape(seq_count * tok_len, 3 * features)
    w_joint = jnp.concatenate([w_query, w_key, w_value], axis=1)
    grad_joint = outer_sum(normed_low, grad_lin_rows)
    grad_norm1 = back_prod(grad_lin_rows, w_joint)
    input_part, grad_gattn = norm_back(
        rows_in, factor_attn, gain_attn.astype(jnp.float32), grad_norm1
    )
    input_grad = grad_resid + input_part
    grads = (
        grad_gattn,
        grad_joint[:, :features],
        grad_joint[:, features : 2 * features],
        grad_joint[:, 2 * features :],
        grad_kernel[:, :features],
        grad_kernel[:, features : 2 * features],
        grad_kernel[:, 2 * features :],
        grad_wout,
        grad_bout,
        grad_gffn,
        grad_wup,
        grad_bup,
        grad_wdown,
        grad_bdown,
    )
    return (grads, input_grad)


def general_shards(
    block_input,
    out_grad,
    prefix_len,
    attn_gain,
    q_weight,
    k_weight,
    v_weight,
    conv_q,
    conv_k,
    conv_v,
    out_weight,
    out_bias,
    ffn_gain,
    up_weight,
    up_bias,
    down_weight,
    down_bias,
):
    micro_count = block_input.shape[0]
    local_shape = block_input.shape[1:]
    offset = lax.axis_index("ctx") * block_input.shape[2]
    outputs = []
    input_grads = []
    totals = ()
    for microstep in range(micro_count):
        weights = (
            lax.all_gather(attn_gain, ("dp", "ctx"), axis=0, tiled=True),
            lax.all_gather(q_weight, ("dp", "ctx"), axis=0, tiled=True),
            lax.all_gather(k_weight, ("dp", "ctx"), axis=0, tiled=True),
            lax.all_gather(v_weight, ("dp", "ctx"), axis=0, tiled=True),
            lax.all_gather(conv_q, ("dp", "ctx"), axis=1, tiled=True),
            lax.all_gather(conv_k, ("dp", "ctx"), axis=1, tiled=True),
            lax.all_gather(conv_v, ("dp", "ctx"), axis=1, tiled=True),
            lax.all_gather(out_weight, ("dp", "ctx"), axis=0, tiled=True),
            lax.all_gather(out_bias, ("dp", "ctx"), axis=0, tiled=True),
            lax.all_gather(ffn_gain, ("dp", "ctx"), axis=0, tiled=True),
            lax.all_gather(up_weight, ("dp", "ctx"), axis=0, tiled=True),
            lax.all_gather(up_bias, ("dp", "ctx"), axis=0, tiled=True),
            lax.all_gather(down_weight, ("dp", "ctx"), axis=0, tiled=True),
            lax.all_gather(down_bias, ("dp", "ctx"), axis=0, tiled=True),
        )
        inputs = block_input[microstep].astype(jnp.float32)
        prefix = prefix_len[microstep]
        saved, result = forward_pass(inputs, prefix, weights, offset)
        weights = (
            lax.all_gather(attn_gain, ("dp", "ctx"), axis=0, tiled=True),
            lax.all_gather(q_weight, ("dp", "ctx"), axis=0, tiled=True),
            lax.all_gather(k_weight, ("dp", "ctx"), axis=0, tiled=True),
            lax.all_gather(v_weight, ("dp", "ctx"), axis=0, tiled=True),
            lax.all_gather(conv_q, ("dp", "ctx"), axis=1, tiled=True),
            lax.all_gather(conv_k, ("dp", "ctx"), axis=1, tiled=True),
            lax.all_gather(conv_v, ("dp", "ctx"), axis=1, tiled=True),
            lax.all_gather(out_weight, ("dp", "ctx"), axis=0, tiled=True),
            lax.all_gather(out_bias, ("dp", "ctx"), axis=0, tiled=True),
            lax.all_gather(ffn_gain, ("dp", "ctx"), axis=0, tiled=True),
            lax.all_gather(up_weight, ("dp", "ctx"), axis=0, tiled=True),
            lax.all_gather(up_bias, ("dp", "ctx"), axis=0, tiled=True),
            lax.all_gather(down_weight, ("dp", "ctx"), axis=0, tiled=True),
            lax.all_gather(down_bias, ("dp", "ctx"), axis=0, tiled=True),
        )
        grads, input_grad = backward_pass(saved, out_grad[microstep], prefix, weights, offset)
        totals = (
            grads
            if microstep == 0
            else tuple((earlier + later for earlier, later in zip(totals, grads)))
        )
        outputs.append(result.astype(jnp.bfloat16).reshape(local_shape))
        input_grads.append(input_grad.reshape(local_shape))
    owned = (
        lax.psum_scatter(totals[0], ("dp", "ctx"), scatter_dimension=0, tiled=True),
        lax.psum_scatter(totals[1], ("dp", "ctx"), scatter_dimension=0, tiled=True),
        lax.psum_scatter(totals[2], ("dp", "ctx"), scatter_dimension=0, tiled=True),
        lax.psum_scatter(totals[3], ("dp", "ctx"), scatter_dimension=0, tiled=True),
        lax.psum_scatter(totals[4], ("dp", "ctx"), scatter_dimension=1, tiled=True),
        lax.psum_scatter(totals[5], ("dp", "ctx"), scatter_dimension=1, tiled=True),
        lax.psum_scatter(totals[6], ("dp", "ctx"), scatter_dimension=1, tiled=True),
        lax.psum_scatter(totals[7], ("dp", "ctx"), scatter_dimension=0, tiled=True),
        lax.psum_scatter(totals[8], ("dp", "ctx"), scatter_dimension=0, tiled=True),
        lax.psum_scatter(totals[9], ("dp", "ctx"), scatter_dimension=0, tiled=True),
        lax.psum_scatter(totals[10], ("dp", "ctx"), scatter_dimension=0, tiled=True),
        lax.psum_scatter(totals[11], ("dp", "ctx"), scatter_dimension=0, tiled=True),
        lax.psum_scatter(totals[12], ("dp", "ctx"), scatter_dimension=0, tiled=True),
        lax.psum_scatter(totals[13], ("dp", "ctx"), scatter_dimension=0, tiled=True),
    )
    return (
        jnp.stack(outputs),
        jnp.stack(input_grads),
        owned[0],
        owned[1],
        owned[2],
        owned[3],
        owned[4],
        owned[5],
        owned[6],
        owned[7],
        owned[8],
        owned[9],
        owned[10],
        owned[11],
        owned[12],
        owned[13],
    )


CHIPS = 4
F32 = jnp.float32
BF16 = jnp.bfloat16


def plane_plan(mesh):
    return mesh.shape["ctx"] == 2 * CHIPS and mesh.shape["dp"] == 4


def dot_nn(left, right):
    return jnp.dot(left, right, preferred_element_type=F32)


def dot_nt(left, right):
    return lax.dot_general(left, right, (((1,), (1,)), ((), ())), preferred_element_type=F32)


def dot_tn(left, right):
    return lax.dot_general(left, right, (((0,), (0,)), ((), ())), preferred_element_type=F32)


def call(body, outs, *args, smem=1, hbm=0, scratch=(), name=None, us=0, room=0):
    out_shape = [jax.ShapeDtypeStruct(shape, dtype) for shape, dtype in outs]
    scratch_shapes = [pltpu.VMEM(*spec) if isinstance(spec, tuple) else spec for spec in scratch]
    size = sum(a.size * a.dtype.itemsize for a in args)
    size += sum(int(jnp.dtype(o.dtype).itemsize) * o.size for o in out_shape)
    for spec in scratch:
        if isinstance(spec, tuple):
            size += int(jnp.dtype(spec[1]).itemsize) * functools.reduce(lambda a, b: a * b, spec[0], 1)
    spaces = [pltpu.SMEM] * smem + [pltpu.VMEM] * (len(args) - smem - hbm) + [pltpu.HBM] * hbm
    return pl.pallas_call(
        body,
        out_shape=out_shape,
        compiler_params=pltpu.CompilerParams(vmem_limit_bytes=room or int(size) + (4 << 20)),
        in_specs=[pl.BlockSpec(memory_space=space) for space in spaces],
        out_specs=[pl.BlockSpec(memory_space=pltpu.VMEM)] * len(outs),
        scratch_shapes=scratch_shapes,
        name=name,
        cost_estimate=pl.CostEstimate(flops=1 + us * 10**9, transcendentals=0, bytes_accessed=1),
    )(*args[: len(args) - hbm], *(pltpu.with_memory_space_constraint(a, pltpu.HBM) for a in args[len(args) - hbm :]))


def send(value, bits):
    dp, ctx = lax.axis_size("dp"), lax.axis_size("ctx")
    pairs = [(i, (i // ctx) * ctx + ((i % ctx) ^ bits)) for i in range(dp * ctx)]
    return lax.ppermute(value, ("dp", "ctx"), pairs)


def send_z(value, bits):
    dp, ctx = lax.axis_size("dp"), lax.axis_size("ctx")
    pairs = [(i, ((i // ctx) ^ bits) * ctx + i % ctx) for i in range(dp * ctx)]
    return lax.ppermute(value, ("dp", "ctx"), pairs)


def after(value, *waits):
    return lax.optimization_barrier((value, *waits))[0]


def all_after(values, *waits):
    return list(lax.optimization_barrier((*values, *waits))[: len(values)])


def to_chips(blocks):
    return [blocks[0]] + [send(blocks[j], 2 * j) for j in range(1, CHIPS)]


def to_all_planes(ids, block, *first, direct=False):
    two, one = send_z(block, 2), send_z(block, 1)
    three = send_z(block, 3) if direct else send_z(after(two, *first), 1)
    return call(stack_k, [((4, *block.shape), block.dtype)], ids, block, one, two, three, name="stack")[0]


def stack_k(ids, s0, s1, s2, s3, out):
    for r, ref in enumerate((s0, s1, s2, s3)):
        out[r] = ref[...]


def join_k(ids, mine, other, keep, later, now):
    n = keep.shape[0]
    for r, out in ((0, keep), (2, later), (1, now.at[0]), (3, now.at[1])):
        at = slice(r * n, r * n + n)
        out[...] = (mine[at].astype(F32) + other[at].astype(F32)).astype(BF16)


def pass_on_k(ids, later, got, out):
    out[...] = (later[...].astype(F32) + got[1].astype(F32)).astype(BF16)


def join_cores(ids, keep, away, name):
    size = (keep.shape[0] // 4, *keep.shape[1:])
    return call(
        join_k, [(size, BF16)] * 2 + [((2, *size), BF16)], ids, keep, send(away, 1), name="join_" + name
    )


def to_all_chips(block):
    half = block.shape[0] // 2
    one, two = send(block, 2), send(block, 4)
    return [block, one, two, send(one[:half], 4), send(two[half:], 2)]


def add_half_k(ids, one, two, low, high, one_out, two_out):
    half = low.shape[0]
    one_out[:half, :] = one[:half, :]
    one_out[half:, :] = (one[half:, :].astype(F32) + high[...].astype(F32)).astype(BF16)
    two_out[half:, :] = two[half:, :]
    two_out[:half, :] = (two[:half, :].astype(F32) + low[...].astype(F32)).astype(BF16)


def to_owners(ids, own, one, two, low, high, *first):
    low, high = all_after([send(low, 2), send(high, 4)], *first)
    one, two = call(add_half_k, [(one.shape, BF16)] * 2, ids, one, two, low, high, name="add_half")
    return own, one, two


ROWS = ((0, 256), (256, 512), (512, 768), (768, 896), (896, 1024))


def place_k(ids, other, mine, out, sem):
    c = ids[2]
    rows = other.shape[2]
    copy = pltpu.make_async_copy(mine.at[c, 0], out.at[pl.ds(pl.multiple_of(c * rows, rows), rows), :], sem)
    copy.start()
    out[pl.ds(pl.multiple_of((1 - c) * rows, rows), rows), :] = other[c, 0]
    copy.wait()


def pack_k(ids, *refs):
    k = ids[1]
    args, (p0, p1, p2, p3), stage, held, sems = refs[:13], refs[13:17], refs[17], refs[18:31], refs[31]
    copies = [pltpu.make_async_copy(ref, to, sems.at[i]) for i, (ref, to) in enumerate(zip(args, held))]
    for copy in copies:
        copy.start()
    for copy in copies:
        copy.wait()
    wq, wk, wv, up, wo, *vectors, bias_u = held
    rows = jnp.concatenate([ref[...].astype(F32).reshape(-1, 24) for ref in vectors], axis=0)
    rows = jnp.concatenate([rows, jnp.zeros((128 - rows.shape[0], 24), F32)], axis=0)
    rows = jnp.concatenate([rows, jnp.zeros((128, 104), F32)], axis=1)
    cols = rows.T[:24, :16]
    bias = bias_u[...].astype(F32).reshape(1, 96)
    bias = jnp.concatenate([bias[:, 24 * i : 24 * i + 24] for i in range(4)] + [jnp.zeros((20, 24), F32)], axis=0)
    tail = jnp.concatenate([cols, bias, jnp.zeros((24, 24), F32)], axis=1).astype(BF16)
    for chip in range(CHIPS):
        lo = 192 * chip
        for part, ref in enumerate((wq, wk, wv)):
            stage[chip, :, 192 * part : 192 * part + 192] = ref[:, lo : lo + 192]
        stage[chip, :, 576:640] = tail
        for plane in range(4):
            at = 640 + 192 * plane
            stage[chip, :, at : at + 192] = up[:, 768 * plane + lo : 768 * plane + lo + 192]
        stage[chip, :, 1408:2176] = wo[...]
    for j, out in enumerate((p0, p1, p2, p3)):
        out[...] = stage[k ^ j]


def split_k(ids, p0, p1, p2, p3, a_out, b_out):
    for j, ref in enumerate((p0, p1, p2, p3)):
        a_out[j] = ref[:, :640]
        b_out[j] = ref[:, 640:1408]
        b_out[CHIPS + j] = ref[:, 1408:2176]


def with_down_k(ids, b, wd, b_out, sems):
    copies = [
        pltpu.make_async_copy(wd.at[24 * j : 24 * j + 24, :], b_out.at[8 + j], sems.at[j]) for j in range(CHIPS)
    ]
    for copy in copies:
        copy.start()
    b_out[0:8] = b[...]
    for copy in copies:
        copy.wait()


def gather_b_k(ids, mine, other, up_out, wo_out, wd_out):
    z, k, c = ids[0], ids[1], ids[2]
    for core, ref in enumerate((mine, other)):
        for plane in range(4):
            for j in range(CHIPS):
                at = (z ^ plane) * 8 + (k ^ j) * 2 + (c ^ core)
                up_out[at] = ref[plane, j]
                wo_out[at] = ref[plane, CHIPS + j]
                wd_out[((z ^ plane) * 2 + (c ^ core)) * 4 + j] = ref[plane, 8 + j]


def hidden_grad_k(ids, g0, g1, g2, g3, g4, wd, dh, g_all):
    for ref, (lo, hi) in zip((g0, g1, g2, g3, g4), ROWS):
        g_all[lo:hi, :] = ref[...]

    def block(j, carry):
        at = pl.ds(pl.multiple_of(256 * j, 256), 256)
        dh[at, :] = dot_nt(g_all[at, :], wd[...]).astype(BF16)
        return carry

    lax.fori_loop(0, 4, block, 0)


def mask_rows(b, prefix, out):
    cols = max(256 * (b + 1), 512)
    row_ids = 256 * b + lax.broadcasted_iota(jnp.int32, (256, cols), 0)
    col_ids = lax.broadcasted_iota(jnp.int32, (256, cols), 1)
    out[:, :cols] = jnp.where((col_ids <= row_ids) | (col_ids < prefix), 0.0, NEG)
    return cols


def attend_k(
    ids, pre, *refs,
):
    pieces, xs = refs[:2], refs[2:6]
    w_out, bias_out, a_out, lin, q_out, k_out, v_out, o0, o1, o2, o3, att, lse, small_out, kern_out = refs[6:21]
    w_scr, stage, mask, mixed = refs[21:]
    z, k, c = ids[0], ids[1], ids[2]
    prefix = pre[c, 0]
    for core in range(2):
        for plane in range(4):
            for j in range(CHIPS):
                w_scr[(z ^ plane) * 8 + (k ^ j) * 2 + (c ^ core)] = pieces[core][plane, j].astype(F32)
    bias_out[...] = jnp.zeros_like(bias_out)
    for plane in range(4):
        for core in range(2):
            piece = w_scr[plane * 8 + k * 2 + core, :, 512:640]
            for part in range(4):
                at = 96 * (2 * plane + core) + 24 * part
                bias_out[0:1, at : at + 24] = piece[part : part + 1, 80:104]
    small = w_scr[:, :, 512:640].reshape(768, 128).T[64:80]
    w_out[...] = w_scr[:, :, 0:576].reshape(768, 576).astype(BF16)
    small_out[...] = small
    gain = small[0:1]
    own = jnp.zeros((9, 192), F32)
    for chip in range(CHIPS):
        own = jnp.where(k == chip, small[1:10, 192 * chip : 192 * chip + 192], own)
    kern = jnp.concatenate([own[0:3], own[3:6], own[6:9]], axis=1)
    kern_out[...] = kern
    lin[0:8, :] = jnp.zeros((8, lin.shape[1]), F32)
    for j, ref in enumerate(xs):
        at = pl.multiple_of((k ^ j) * 256, 256)
        x = ref[...].astype(F32)
        factor = lax.rsqrt(jnp.mean(x * x, axis=-1, keepdims=True) + EPS)
        a_out[pl.ds(at, 256), :] = (x * factor * gain).astype(BF16)

    def project(b, carry):
        at = pl.multiple_of(256 * b, 256)
        lin[pl.ds(pl.multiple_of(at + 8, 8), 256), :] = dot_nn(a_out[pl.ds(at, 256), :], w_out[...])
        return carry

    lax.fori_loop(0, 4, project, 0)
    for b in range(4):
        t = 256 * b
        mixed[...] = (
            kern[0:1] * lin[8 + t : 264 + t, :]
            + kern[1:2] * lin[7 + t : 263 + t, :]
            + kern[2:3] * lin[6 + t : 262 + t, :]
        ).astype(BF16)
        for h in range(3):
            lo = 64 * h
            q_out[h, t : t + 256, :] = mixed[:, lo : lo + 64] * BF16(HEAD ** (-0.5))
            k_out[h, t : t + 256, :] = mixed[:, 192 + lo : 256 + lo]
            v_out[h, t : t + 256, :] = mixed[:, 384 + lo : 448 + lo]
    for b in range(4):
        t = 256 * b
        cols = mask_rows(b, prefix, mask)

        def one_head(h, carry, t=t, cols=cols):
            scores = dot_nt(q_out[h, t : t + 256, :], k_out[h, 0:cols, :]) + mask[:, :cols]
            top = jnp.max(scores, axis=-1, keepdims=True)
            weight = jnp.exp(scores - top)
            total = jnp.sum(weight, axis=-1, keepdims=True)
            probs = (weight * (1.0 / total)).astype(BF16)
            att[h, t : t + 256, :] = dot_nn(probs, v_out[h, 0:cols, :])
            lse[h, t : t + 256, :] = top + jnp.log(total)
            return carry

        lax.fori_loop(0, 3, one_head, 0)
        stage[b] = jnp.concatenate([att[h, t : t + 256, :] for h in range(3)], axis=1).astype(BF16)
    for j, out in enumerate((o0, o1, o2, o3)):
        out[...] = stage[k ^ j]


def resid_k(ids, t0, t1, t2, t3, wo, xw, small, x1_out, a2_out):
    k = ids[1]
    total = xw[...].astype(F32) + small[10:11]
    for j, ref in enumerate((t0, t1, t2, t3)):
        at = pl.multiple_of((k ^ j) * 192, 192)
        total = total + dot_nn(ref[...], wo[pl.ds(at, 192), :])
    x1_out[...] = total
    factor = lax.rsqrt(jnp.mean(total * total, axis=-1, keepdims=True) + EPS)
    a2_out[...] = (total * factor * small[11:12]).astype(BF16)


def ffn_k(ids, a0, a1, a2, a3, a4, dh, up, bias, hsq, du, a_all, p0, p1, p2, p3, p4, stage):
    for ref, (lo, hi) in zip((a0, a1, a2, a3, a4), ROWS):
        a_all[lo:hi, :] = ref[...]

    def block(j, carry):
        at = pl.ds(pl.multiple_of(256 * j, 256), 256)
        act = jax.nn.relu(dot_nn(a_all[at, :], up[...]) + bias[...])
        hsq[at, :] = (act * act).astype(BF16)
        low = (dh[at, :].astype(F32) * 2.0 * act).astype(BF16)
        du[at, :] = low
        stage[at, :] = dot_nt(low, up[...]).astype(BF16)
        return carry

    lax.fori_loop(0, 4, block, 0)
    for ref, (lo, hi) in zip((p0, p1, p2, p3, p4), ROWS):
        ref[...] = stage[lo:hi, :]


def ffn_out_k(ids, hsq, wd, p0, p1, p2, p3):
    for j, out in enumerate((p0, p1, p2, p3)):
        out[...] = dot_nn(hsq[256 * j : 256 * j + 256, :], wd[...]).astype(BF16)


def ffn_grads_k(ids, a_all, g_all, hsq, du, keep, away, bias_out, stage):
    z, k, c = ids[0], ids[1], ids[2]
    bias_out[...] = jnp.sum(du[...].astype(F32), axis=0, keepdims=True)
    up_grad = dot_tn(a_all[...], du[...])
    for plane in range(4):
        for core in range(2):
            to, at = c ^ core, (z ^ plane) * 8
            for chip in range(CHIPS):
                row = 24 * (plane * 8 + chip * 2 + core)
                stage[to, at + (k ^ chip)] = up_grad[row : row + 24].astype(BF16)
    down_grad = dot_tn(hsq[...], g_all[...])
    for plane in range(4):
        for core in range(2):
            to, at = c ^ core, (z ^ plane) * 8
            for chip in range(CHIPS):
                row = 96 * (plane * 2 + core) + 24 * chip
                stage[to, at + 4 + chip] = down_grad[row : row + 24].astype(BF16)
    keep[...] = stage[0]
    away[...] = stage[1]


def sum_planes_k(ids, *refs):
    f, o, r, (d_out, *outs) = refs[0:3], refs[3:6], refs[6:9], refs[9:]

    def total(parts, at):
        return parts[0][at].astype(F32) + parts[1][0, at].astype(F32) + parts[2][at].astype(F32)

    for j, out in enumerate(outs):
        out[:, 0:640] = total(r, j).astype(BF16)
        out[:, 640:1408] = total(f, j).astype(BF16)
        out[:, 1408:2176] = total(o, j).astype(BF16)
        d_out[24 * j : 24 * j + 24, :] = total(f, CHIPS + j)


def mid_grad_k(
    ids, p0, p1, p2, x1, gw, small, wo, dx_out, dz_out, bias_out, o0, o1, o2, o3
):
    k = ids[1]
    da2 = p0[...].astype(F32) + p1[...].astype(F32) + p2[...].astype(F32)
    val = x1[...]
    factor = lax.rsqrt(jnp.mean(val * val, axis=-1, keepdims=True) + EPS)
    weighted = da2 * small[11:12]
    inner = jnp.mean(weighted * val, axis=-1, keepdims=True)
    dx = gw[...].astype(F32) + factor * weighted - val * (factor * factor * factor * inner)
    dx_out[...] = dx
    low = dx.astype(BF16)
    dz_out[...] = low
    bias_out[...] = jnp.sum(low.astype(F32), axis=0, keepdims=True)
    for j, out in enumerate((o0, o1, o2, o3)):
        at = pl.multiple_of((k ^ j) * 192, 192)
        out[...] = dot_nt(low, wo[pl.ds(at, 192), :]).astype(BF16)


def out_grads_k(ids, t0, t1, t2, t3, dz, keep, away, stage):
    z, k, c = ids[0], ids[1], ids[2]
    for j, ref in enumerate((t0, t1, t2, t3)):
        part = dot_tn(ref[...], dz[...])
        at = ((k ^ j) ^ z) * 4
        for chip in range(CHIPS):
            for core in range(2):
                row = 24 * (2 * chip + core)
                stage[c ^ core, at + (k ^ chip)] = part[row : row + 24].astype(BF16)
    keep[...] = stage[0]
    away[...] = stage[1]


def attend_grad_k(
    ids, pre, d0, d1, d2, d3, q_in, k_in, v_in, att, lse, lin, kern, w,
    dlin_out, conv_out, p0, p1, p2, p3, p4, do_scr, dm, mask, dq, dk, dv, stage,
):
    k, c = ids[1], ids[2]
    prefix = pre[c, 0]
    for j, ref in enumerate((d0, d1, d2, d3)):
        for h in range(3):
            do_scr[h, pl.ds(pl.multiple_of((k ^ j) * 256, 256), 256), :] = ref[:, 64 * h : 64 * h + 64]
    dm[1024:1032, :] = jnp.zeros((8, 576), F32)
    for b in (3, 2, 1, 0):
        t = 256 * b
        cols = mask_rows(b, prefix, mask)

        def one_head(h, carry, b=b, t=t, cols=cols):
            q_rows, do_rows = q_in[h, t : t + 256, :], do_scr[h, t : t + 256, :]
            scores = dot_nt(q_rows, k_in[h, 0:cols, :]) + mask[:, :cols]
            probs = jnp.exp(scores - lse[h, t : t + 256, :])
            delta = jnp.sum(do_rows.astype(F32) * att[h, t : t + 256, :], axis=-1, keepdims=True)
            dprobs = dot_nt(do_rows, v_in[h, 0:cols, :])
            dscores = (probs * (dprobs - delta)).astype(BF16)
            dq[h, t : t + 256, :] = dot_nn(dscores, k_in[h, 0:cols, :]) * HEAD ** (-0.5)
            dk_part = dot_tn(q_rows, dscores)
            dv_part = dot_tn(do_rows, probs.astype(BF16))
            if b == 3:
                dk[h] = dk_part
                dv[h] = dv_part
            else:
                dk[h, :, 0:cols] = dk[h, :, 0:cols] + dk_part
                dv[h, :, 0:cols] = dv[h, :, 0:cols] + dv_part
            return carry

        lax.fori_loop(0, 3, one_head, 0)
    for h in range(3):
        dm[0:1024, 64 * h : 64 * h + 64] = dq[h]
        dm[0:1024, 192 + 64 * h : 256 + 64 * h] = dk[h].T
        dm[0:1024, 384 + 64 * h : 448 + 64 * h] = dv[h].T
    taps = kern[...]
    sums = [jnp.zeros((1, 576), F32) for _ in range(3)]
    for b in range(4):
        t = 256 * b
        here = dm[t : t + 256, :]
        dlin_out[t : t + 256, :] = (
            taps[0:1] * here + taps[1:2] * dm[t + 1 : t + 257, :] + taps[2:3] * dm[t + 2 : t + 258, :]
        ).astype(BF16)
        for back in range(3):
            sums[back] = sums[back] + jnp.sum(
                here * lin[8 - back + t : 264 - back + t, :], axis=0, keepdims=True
            )
    conv_out[...] = jnp.concatenate(sums, axis=0)

    def block(j, carry):
        rows = dlin_out[pl.ds(pl.multiple_of((k ^ j) * 256, 256), 256), :]
        stage[pl.ds(pl.multiple_of(256 * j, 256), 256), :] = dot_nt(rows, w[...]).astype(BF16)
        return carry

    lax.fori_loop(0, 4, block, 0)
    for ref, (lo, hi) in zip((p0, p1, p2, p3, p4), ROWS):
        ref[...] = stage[lo:hi, :]


def proj_grads_k(ids, a1, dlin, conv, up_bias, out_bias, g, keep, away, stage):
    z, k, c = ids[0], ids[1], ids[2]
    grad = dot_tn(a1[...], dlin[...])
    conv_rows = jnp.concatenate([conv[:, 0:192], conv[:, 192:384], conv[:, 384:576]], axis=0)
    conv_all = jnp.concatenate(
        [jnp.where(k == chip, conv_rows, 0.0) for chip in range(CHIPS)], axis=1
    )
    down_bias = jnp.sum(g[...].astype(F32), axis=0, keepdims=True)
    rows = jnp.concatenate(
        [conv_all, out_bias[...], down_bias, jnp.zeros((117, 768), F32)], axis=0
    )
    cols = rows.T
    for plane in range(4):
        for chip in range(CHIPS):
            for core in range(2):
                row = 24 * (plane * 8 + chip * 2 + core)
                to, at = c ^ core, (z ^ plane) * 4 + (k ^ chip)
                stage[to, at, :, 0:576] = grad[row : row + 24]
                stage[to, at, :, 576:640] = cols[row : row + 24, 0:64]
    for plane in range(4):
        for core in range(2):
            for part in range(4):
                lo = 96 * (2 * plane + core) + 24 * part
                stage[c ^ core, (z ^ plane) * 4, part : part + 1, 592:616] = up_bias[0:1, lo : lo + 24]
    keep[...] = stage[0].astype(BF16)
    away[...] = stage[1].astype(BF16)


def halves_k(ids, total_fn, keep, away):
    c = ids[2]
    keep[...] = total_fn(pl.ds(pl.multiple_of(c * 128, 128), 128)).astype(keep.dtype)
    away[...] = total_fn(pl.ds(pl.multiple_of((1 - c) * 128, 128), 128)).astype(away.dtype)


def output_k(ids, p0, p1, p2, p3, x1, small, keep, away):
    def rows_of(at):
        total = p0[at, :].astype(F32) + p1[at, :].astype(F32) + p2[at, :].astype(F32)
        return x1[at, :] + (total + p3[at, :].astype(F32)) + small[12:13]

    halves_k(ids, rows_of, keep, away)


def input_grad_k(ids, p0, p1, p2, xw, dx, small, keep, away):
    def rows_of(at):
        da1 = p0[at, :].astype(F32) + p1[at, :].astype(F32) + p2[at, :].astype(F32)
        val = xw[at, :].astype(F32)
        factor = lax.rsqrt(jnp.mean(val * val, axis=-1, keepdims=True) + EPS)
        weighted = da1 * small[0:1]
        inner = jnp.mean(weighted * val, axis=-1, keepdims=True)
        return dx[at, :] + factor * weighted - val * (factor * factor * factor * inner)

    halves_k(ids, rows_of, keep, away)


def deliver_k(ids, out_keep, out_recv, in_keep, in_recv, out_ref, in_ref):
    c = ids[2]
    out_ref[c, 0] = out_keep[...]
    out_ref[1 - c, 0] = out_recv[...]
    in_ref[c, 0] = in_keep[...]
    in_ref[1 - c, 0] = in_recv[...]


def owned_k(
    ids, s0, s1, s2, s3, wq, wk, wv, up, gain_a, gain_f,
    gq, gk, gv, cq, ck, cv, go, gu, ga, gf, bo, bd, bu, stage_r, stage_u,
):
    k = ids[1]
    extra = jnp.zeros((24, 128), F32)
    out_sum = jnp.zeros((24, 768), F32)
    for j, ref in enumerate((s0, s1, s2, s3)):
        stage_r[k ^ j] = ref[:, 0:640].astype(F32)
        stage_u[k ^ j] = ref[:, 640:1408].astype(F32)
        out_sum = out_sum + ref[:, 1408:2176].astype(F32)
        extra = extra + ref[:, 512:640].astype(F32)
    go[...] = out_sum
    for chip in range(CHIPS):
        lo = 192 * chip
        for part, ref in enumerate((gq, gk, gv)):
            ref[:, lo : lo + 192] = stage_r[chip, :, 192 * part : 192 * part + 192]
        for plane in range(4):
            at = 768 * plane + lo
            gu[:, at : at + 192] = stage_u[chip, :, 192 * plane : 192 * plane + 192]
    attn = jnp.sum(
        gq[...] * wq[...].astype(F32) + gk[...] * wk[...].astype(F32) + gv[...] * wv[...].astype(F32),
        axis=-1, keepdims=True,
    )
    ffn = jnp.sum(gu[...] * up[...].astype(F32), axis=-1, keepdims=True)
    cols = jnp.concatenate([extra[:, 64:75], attn, ffn, jnp.zeros((24, 115), F32)], axis=1)
    cols = jnp.concatenate([cols, jnp.zeros((104, 128), F32)], axis=0)
    rows = cols.T[:16, :24]
    for at, ref in ((0, cq), (3, ck), (6, cv)):
        ref[...] = rows[at : at + 3]
    bo[...] = rows[9]
    bd[...] = rows[10]
    ga[...] = rows[11] / gain_a[...].astype(F32)
    gf[...] = rows[12] / gain_f[...].astype(F32)
    bu[...] = jnp.concatenate([extra[i : i + 1, 80:104] for i in range(4)], axis=1).reshape(96)


def plane_shards(
    block_input, out_grad, prefix_len, attn_gain, q_weight, k_weight, v_weight, conv_q, conv_k, conv_v,
    out_weight, out_bias, ffn_gain, up_weight, up_bias, down_weight, down_bias,
):
    z, place = lax.axis_index("dp"), lax.axis_index("ctx")
    ids = jnp.stack([z, place // 2, place % 2]).astype(jnp.int32)
    block, half = ((256, 768), BF16), ((128, 768), BF16)
    blocks = [block] * 3 + [half] * 2
    tall, heads = ((1024, 768), BF16), (3, 1024, 64)

    sem = pltpu.SemaphoreType.DMA
    x_peer = send(block_input, 1)
    weights = (
        q_weight, k_weight, v_weight, up_weight, out_weight, attn_gain, conv_q, conv_k, conv_v, out_bias,
        ffn_gain, down_bias, up_bias,
    )
    packs = call(
        pack_k, [((24, 2176), BF16)] * 4, ids, *weights, hbm=13,
        scratch=[((4, 24, 2176), BF16)] + [(w.shape, BF16) for w in weights] + [sem((13,))], name="pack",
    )
    packs = to_chips(packs)
    x_peer = after(x_peer, *packs[1:])
    (xw,) = call(place_k, [block], ids, x_peer, block_input, hbm=1, scratch=[sem(())], name="place_x")
    xs = to_chips([xw] * 4)
    a_own, b_own = call(split_k, [((4, 24, 640), BF16), ((8, 24, 768), BF16)], ids, *packs, name="split")
    a_two, a_one = send_z(a_own, 2), send_z(a_own, 1)
    a_three = send_z(a_two, 1)
    (b_own,) = call(
        with_down_k, [((12, 24, 768), BF16)], ids, after(b_own, a_two), down_weight, hbm=1, scratch=[sem((4,))],
        name="with_down",
    )

    g_peer = send(after(out_grad, *packs[1:]), 1)
    (gw,) = call(place_k, [block], ids, g_peer, out_grad, hbm=1, scratch=[sem(())], name="place_g")
    (a_all,) = call(stack_k, [((4, 4, 24, 640), BF16)], ids, a_own, a_one, a_two, after(a_three, b_own, gw), name="stack_a")
    a_peer = send(a_all, 1)
    b_own = after(b_own, a_three)
    b_one, b_two = send_z(b_own, 1), send_z(b_own, 2)
    gw = after(gw, *xs[1:])
    g_one, g_two = send(gw, 2), send(gw, 4)

    w_a, up_bias_row, a1, lin, q, k, v, t0, t1, t2, t3, att, lse, small, kern = call(
        attend_k,
        [((768, 576), BF16), ((1, 768), F32), tall, ((1032, 576), F32)]
        + [(heads, BF16)] * 3 + [((256, 192), BF16)] * 4
        + [(heads, F32), ((3, 1024, 1), F32), ((16, 768), F32), ((3, 576), F32)],
        ids, prefix_len, after(a_all, gw), a_peer, *xs,
        smem=2, name="attend", us=0,
        scratch=[((32, 24, 640), F32), ((4, 256, 192), BF16), ((256, 1024), F32), ((256, 576), BF16)],
    )
    atts = [t0, send(t1, 2), send(t2, 4)]
    atts.append(send(after(t3, atts[1]), 6))
    b_one, b_two, g_one, g_two = all_after([b_one, b_two, g_one, g_two], t1)
    b_three = send_z(b_two, 1)
    g_low, g_high = send(g_one[:128], 4), send(g_two[128:], 2)
    (b_all,) = call(
        stack_k, [((4, 12, 24, 768), BF16)], ids, b_own, *all_after([b_one, b_two, b_three], *atts[1:3], g_low, g_high), name="stack_b"
    )
    w_up, w_o, w_d = [
        w.reshape(768, 768)
        for w in call(gather_b_k, [((32, 24, 768), BF16)] * 3, ids, b_all, send(b_all, 1), name="gather_b")
    ]
    x1, a2 = call(resid_k, [((256, 768), F32), block], ids, *atts, w_o, xw, small, name="resid")
    a2s = to_all_chips(a2)
    dh, g_all = call(hidden_grad_k, [tall] * 2, ids, gw, g_one, g_two, g_low, g_high, w_d, name="hidden_grad")
    hsq, du, a2_all, *da2 = call(
        ffn_k, [tall] * 3 + blocks, ids, *a2s, dh, w_up, up_bias_row, scratch=[tall], name="ffn"
    )
    da2, da2_one, da2_two = to_owners(ids, *da2)
    da2 = [da2, send(da2_one, 2), send(da2_two, 4)]
    hsq, du = all_after([hsq, du], da2_one)
    f_keep, f_away, up_bias_grad = call(
        ffn_grads_k, [((32, 24, 768), BF16)] * 2 + [((1, 768), F32)], ids, a2_all, g_all, hsq, du,
        scratch=[((2, 32, 24, 768), BF16)], name="ffn_grads", us=100,
    )
    f_keep, f_later, f_now = join_cores(ids, f_keep, f_away, "f")
    f_now = send_z(f_now, 1)

    outs = call(ffn_out_k, [block] * 4, ids, hsq, w_d, name="ffn_out", us=100)
    dx, dz, out_bias_grad, *datt = call(
        mid_grad_k, [((256, 768), F32), block, ((1, 768), F32)] + [((256, 192), BF16)] * 4,
        ids, *da2, x1, after(gw, f_keep, outs[0]), small, w_o, name="mid_grad",
    )
    datt = to_chips(datt)
    o_keep, o_away = call(
        out_grads_k, [((16, 24, 768), BF16)] * 2, ids, *atts, dz,
        scratch=[((2, 16, 24, 768), BF16)], name="out_grads", us=0,
    )
    out_one, out_two, out_three = all_after(outs[1:], *datt[1:])
    out_one, out_two = send(out_one, 2), send(out_two, 4)
    f_now = after(f_now, *datt[1:])
    (f_later,) = call(pass_on_k, [(f_later.shape, BF16)], ids, f_later, f_now, name="pass_f")
    f_sent = send_z(f_later, 2)
    dlin, conv_grad, *da1 = call(
        attend_grad_k, [((1024, 576), BF16), ((3, 576), F32)] + blocks,
        ids, prefix_len, *datt, after(q, f_later), k, v, att, lse, lin, kern, w_a, smem=2, name="attend_grad", us=1000,
        scratch=[(heads, BF16), ((1032, 576), F32), ((256, 1024), F32), (heads, F32)]
        + [((3, 64, 1024), F32)] * 2 + [tall],
    )
    outs = [outs[0], out_one, out_two, send(after(out_three, dlin), 6)]
    o_keep, o_later, o_now = join_cores(ids, o_keep, after(o_away, dlin), "o")
    o_now = send_z(o_now, 1)
    r_keep, r_away = call(
        proj_grads_k, [((16, 24, 640), BF16)] * 2, ids, after(a1, out_one, out_two, f_sent), dlin, conv_grad, up_bias_grad, out_bias_grad, gw,
        scratch=[((2, 16, 24, 640), F32)], name="proj_grads", us=0,
    )
    da1, da1_one, da1_two = to_owners(ids, *da1)
    da1 = [da1, send(da1_one, 2), send(da1_two, 4)]
    r_keep, r_later, r_now = join_cores(ids, r_keep, r_away, "r")
    r_now = send_z(r_now, 1)
    (o_later,) = call(pass_on_k, [(o_later.shape, BF16)], ids, after(o_later, r_keep), o_now, name="pass_o")
    o_sent = send_z(o_later, 2)
    (r_later,) = call(pass_on_k, [(r_later.shape, BF16)], ids, r_later, r_now, name="pass_r")
    rows = (128, 768)
    out_keep, out_away = call(output_k, [(rows, BF16)] * 2, ids, *outs, after(x1, r_later), small, name="output")
    o_parts = [o_keep, o_now, o_sent]
    f_parts = [f_keep, f_now, f_sent]
    r_parts = [r_keep, r_now, send_z(r_later, 2)]
    down_grad, *sums = call(
        sum_planes_k, [((96, 768), F32)] + [((24, 2176), BF16)] * 4, ids, *f_parts, *o_parts, *r_parts,
        name="sum_planes",
    )
    sums = to_chips(sums)

    out_recv = send(out_away, 1)
    in_keep, in_away = call(input_grad_k, [(rows, F32)] * 2, ids, *da1, xw, after(dx, out_keep), small, name="input_grad")
    in_recv = send(in_away, 1)
    block_output, input_grad = call(
        deliver_k, [((2, 1, 128, 768), BF16), ((2, 1, 128, 768), F32)],
        ids, out_keep, out_recv, in_keep, in_recv, name="deliver", us=100,
    )
    vec = ((24,), F32)
    gq, gk, gv, cq, ck, cv, go, gu, ga, gf, bo, bd, bu = call(
        owned_k,
        [((24, 768), F32)] * 3 + [((3, 24), F32)] * 3 + [((24, 768), F32), ((24, 3072), F32)]
        + [vec] * 4 + [((96,), F32)],
        ids, *sums, q_weight, k_weight, v_weight, up_weight, attn_gain, ffn_gain,
        scratch=[((4, 24, 640), F32), ((4, 24, 768), F32)], name="owned", us=100,
    )
    return (
        block_output, input_grad, ga, gq, gk, gv, cq, ck, cv, go, bo, gf, gu, bu, down_grad, bd,
    )


def solution(mesh):
    plan = plane_shards if plane_plan(mesh) else general_shards
    in_specs = (
        P(None, "dp", "ctx", None),
        P(None, "dp", "ctx", None),
        P(None, "dp"),
        P(("dp", "ctx")),
        P(("dp", "ctx"), None),
        P(("dp", "ctx"), None),
        P(("dp", "ctx"), None),
        P(None, ("dp", "ctx")),
        P(None, ("dp", "ctx")),
        P(None, ("dp", "ctx")),
        P(("dp", "ctx"), None),
        P(("dp", "ctx")),
        P(("dp", "ctx")),
        P(("dp", "ctx"), None),
        P(("dp", "ctx")),
        P(("dp", "ctx"), None),
        P(("dp", "ctx")),
    )
    out_specs = (
        P(None, "dp", "ctx", None),
        P(None, "dp", "ctx", None),
        P(("dp", "ctx")),
        P(("dp", "ctx"), None),
        P(("dp", "ctx"), None),
        P(("dp", "ctx"), None),
        P(None, ("dp", "ctx")),
        P(None, ("dp", "ctx")),
        P(None, ("dp", "ctx")),
        P(("dp", "ctx"), None),
        P(("dp", "ctx")),
        P(("dp", "ctx")),
        P(("dp", "ctx"), None),
        P(("dp", "ctx")),
        P(("dp", "ctx"), None),
        P(("dp", "ctx")),
    )
    return jax.shard_map(plan, mesh=mesh, in_specs=in_specs, out_specs=out_specs, check_vma=False)
```

```python
import functools

import jax
import jax.numpy as jnp
from jax import lax
from jax.experimental import pallas as pl
from jax.experimental.pallas import tpu as pltpu
from jax.sharding import PartitionSpec as P

HEADS = 12
HEAD = 64


EPS = 1e-06
NEG = -1e30


def shifted(shard, axis, by):
    peers = lax.axis_size(axis)
    pairs = [(i, i + by) for i in range(peers) if 0 <= i + by < peers]
    return lax.ppermute(shard, axis, pairs)


def norm_rows(values, gain_vec):
    factor = lax.rsqrt(jnp.mean(values * values, axis=-1, keepdims=True) + EPS)
    return (factor, values * factor * gain_vec)


def norm_back(values, factor, gain_vec, grad_out):
    weighted = grad_out * gain_vec
    inner = jnp.mean(weighted * values, axis=-1, keepdims=True)
    return (
        factor * weighted - values * factor**3 * inner,
        jnp.sum(grad_out * values * factor, axis=0),
    )


def outer_sum(left, right):
    return lax.dot_general(
        left, right, (((0,), (0,)), ((), ())), preferred_element_type=jnp.float32
    )


def back_prod(grad_rows, weight):
    return lax.dot_general(
        grad_rows, weight, (((1,), (1,)), ((), ())), preferred_element_type=jnp.float32
    )


def scores_of(query, key_part, key_start, offset, prefix):
    raw_scores = jnp.einsum("sthe,skhe->shtk", query, key_part, preferred_element_type=jnp.float32)
    row_ids = offset + jnp.arange(query.shape[1], dtype=jnp.int32)
    col_ids = key_start + jnp.arange(key_part.shape[1], dtype=jnp.int32)
    allowed = (col_ids[None, None, :] <= row_ids[None, :, None]) | (
        col_ids[None, None, :] < prefix[:, None, None]
    )
    return jnp.where(allowed[:, None], raw_scores * HEAD ** (-0.5), NEG)


def forward_pass(inputs, prefix, weights, offset):
    (
        gain_attn,
        w_query,
        w_key,
        w_value,
        conv_query,
        conv_key,
        conv_value,
        w_out,
        b_out,
        gain_ffn,
        w_up,
        b_up,
        w_down,
        b_down,
    ) = weights
    seq_count, tok_len, features = inputs.shape
    length = tok_len * lax.axis_size("ctx")
    key_block = min(512, length)
    block_count = length // key_block
    rows_in = inputs.reshape(seq_count * tok_len, features)
    factor_attn, normed = norm_rows(rows_in, gain_attn.astype(jnp.float32))
    normed_low = normed.astype(jnp.bfloat16)
    w_joint = jnp.concatenate([w_query, w_key, w_value], axis=1)
    kernel = jnp.concatenate([conv_query, conv_key, conv_value], axis=1).astype(jnp.float32)
    linear = jnp.dot(normed_low, w_joint, preferred_element_type=jnp.float32).reshape(
        seq_count, tok_len, 3 * features
    )
    before = shifted(linear[:, tok_len - 2 :], "ctx", 1)
    padded = jnp.concatenate([before, linear], axis=1)
    mixed = (
        kernel[0] * padded[:, 2:]
        + kernel[1] * padded[:, 1 : tok_len + 1]
        + kernel[2] * padded[:, :tok_len]
    ).astype(jnp.bfloat16)
    query = mixed[:, :, :features].reshape(seq_count, tok_len, HEADS, HEAD)
    keys_all, values_all = (
        lax.all_gather(mixed[:, :, features : 2 * features], "ctx", axis=1, tiled=True),
        lax.all_gather(mixed[:, :, 2 * features :], "ctx", axis=1, tiled=True),
    )
    keys_all = keys_all.reshape(seq_count, length, HEADS, HEAD)
    values_all = values_all.reshape(seq_count, length, HEADS, HEAD)
    block_ids = jnp.arange(block_count, dtype=jnp.int32)

    def max_turn(carry, key_index):
        row_top, row_total = carry
        key_start = key_index * key_block
        key_part = lax.dynamic_slice_in_dim(keys_all, key_start, key_block, 1)
        scores = scores_of(query, key_part, key_start, offset, prefix)
        new_top = jnp.maximum(row_top, jnp.max(scores, axis=-1))
        row_total = row_total * jnp.exp(row_top - new_top) + jnp.sum(
            jnp.exp(scores - new_top[..., None]), axis=-1
        )
        return ((new_top, row_total), None)

    stat_shape = (seq_count, HEADS, tok_len)
    (row_top, row_total), unused = lax.scan(
        max_turn,
        (jnp.full(stat_shape, NEG, jnp.float32), jnp.zeros(stat_shape, jnp.float32)),
        block_ids,
    )
    log_total = row_top + jnp.log(row_total)

    def out_turn(summed, key_index):
        key_start = key_index * key_block
        key_part = lax.dynamic_slice_in_dim(keys_all, key_start, key_block, 1)
        value_part = lax.dynamic_slice_in_dim(values_all, key_start, key_block, 1)
        scores = scores_of(query, key_part, key_start, offset, prefix)
        probs = jnp.exp(scores - log_total[..., None]).astype(jnp.bfloat16)
        return (
            summed
            + jnp.einsum("shtk,skhe->sthe", probs, value_part, preferred_element_type=jnp.float32),
            None,
        )

    attended, unused = lax.scan(out_turn, jnp.zeros(query.shape, jnp.float32), block_ids)
    attn_low = attended.astype(jnp.bfloat16).reshape(seq_count * tok_len, features)
    resid = rows_in + (
        jnp.dot(attn_low, w_out, preferred_element_type=jnp.float32) + b_out.astype(jnp.float32)
    )
    factor_ffn, normed2 = norm_rows(resid, gain_ffn.astype(jnp.float32))
    normed_ffn = normed2.astype(jnp.bfloat16)
    pre_act = jnp.dot(normed_ffn, w_up, preferred_element_type=jnp.float32) + b_up.astype(
        jnp.float32
    )
    hidden_low = jnp.square(jax.nn.relu(pre_act)).astype(jnp.bfloat16)
    result = (
        resid
        + jnp.dot(hidden_low, w_down, preferred_element_type=jnp.float32)
        + b_down.astype(jnp.float32)
    )
    saved = (
        rows_in,
        factor_attn,
        normed_low,
        padded,
        query,
        keys_all,
        values_all,
        log_total,
        attended,
        attn_low,
        resid,
        factor_ffn,
        normed_ffn,
        pre_act,
        hidden_low,
    )
    return (saved, result)


def backward_pass(saved, cot_low, prefix, weights, offset):
    (
        rows_in,
        factor_attn,
        normed_low,
        padded,
        query,
        keys_all,
        values_all,
        log_total,
        attended,
        attn_low,
        resid,
        factor_ffn,
        normed_ffn,
        pre_act,
        hidden_low,
    ) = saved
    (
        gain_attn,
        w_query,
        w_key,
        w_value,
        conv_query,
        conv_key,
        conv_value,
        w_out,
        b_out,
        gain_ffn,
        w_up,
        b_up,
        w_down,
        b_down,
    ) = weights
    seq_count, tok_len = (query.shape[0], query.shape[1])
    features = rows_in.shape[1]
    length = keys_all.shape[1]
    key_block = min(512, length)
    block_count = length // key_block
    cot_rows = cot_low.reshape(seq_count * tok_len, features)
    cot_full = cot_rows.astype(jnp.float32)
    grad_bdown = jnp.sum(cot_full, axis=0)
    grad_wdown = outer_sum(hidden_low, cot_rows)
    grad_hidden = back_prod(cot_rows, w_down).astype(jnp.bfloat16)
    grad_pre = (grad_hidden.astype(jnp.float32) * 2.0 * jax.nn.relu(pre_act)).astype(jnp.bfloat16)
    grad_bup = jnp.sum(grad_pre.astype(jnp.float32), axis=0)
    grad_wup = outer_sum(normed_ffn, grad_pre)
    grad_normed = back_prod(grad_pre, w_up)
    resid_part, grad_gffn = norm_back(resid, factor_ffn, gain_ffn.astype(jnp.float32), grad_normed)
    grad_resid = cot_full + resid_part
    grad_branch = grad_resid.astype(jnp.bfloat16)
    grad_bout = jnp.sum(grad_branch.astype(jnp.float32), axis=0)
    grad_wout = outer_sum(attn_low, grad_branch)
    grad_attn = (
        back_prod(grad_branch, w_out).astype(jnp.bfloat16).reshape(seq_count, tok_len, HEADS, HEAD)
    )
    delta = jnp.einsum("sthe,sthe->sht", grad_attn.astype(jnp.float32), attended)
    block_ids = jnp.arange(block_count, dtype=jnp.int32)

    def grad_terms(key_index):
        key_start = key_index * key_block
        key_part = lax.dynamic_slice_in_dim(keys_all, key_start, key_block, 1)
        value_part = lax.dynamic_slice_in_dim(values_all, key_start, key_block, 1)
        scores = scores_of(query, key_part, key_start, offset, prefix)
        probs = jnp.exp(scores - log_total[..., None])
        grad_probs = jnp.einsum(
            "sthe,skhe->shtk", grad_attn, value_part, preferred_element_type=jnp.float32
        )
        grad_scores = (probs * (grad_probs - delta[..., None]) * HEAD ** (-0.5)).astype(
            jnp.bfloat16
        )
        return (key_part, probs, grad_scores)

    def back_turn(summed, key_index):
        key_part, probs, grad_scores = grad_terms(key_index)
        summed = summed + jnp.einsum(
            "shtk,skhe->sthe", grad_scores, key_part, preferred_element_type=jnp.float32
        )
        grad_keys = jnp.einsum(
            "shtk,sthe->skhe", grad_scores, query, preferred_element_type=jnp.float32
        )
        grad_values = jnp.einsum(
            "shtk,sthe->skhe",
            probs.astype(jnp.bfloat16),
            grad_attn,
            preferred_element_type=jnp.float32,
        )
        return (summed, (grad_keys, grad_values))

    grad_query, (grad_keys, grad_values) = lax.scan(
        back_turn, jnp.zeros(query.shape, jnp.float32), block_ids
    )
    grad_keys = jnp.moveaxis(grad_keys, 0, 1).reshape(seq_count, length, features)
    grad_values = jnp.moveaxis(grad_values, 0, 1).reshape(seq_count, length, features)
    own_keys, own_values = (
        lax.psum_scatter(
            grad_keys.astype(jnp.bfloat16), "ctx", scatter_dimension=1, tiled=True
        ).astype(jnp.float32),
        lax.psum_scatter(
            grad_values.astype(jnp.bfloat16), "ctx", scatter_dimension=1, tiled=True
        ).astype(jnp.float32),
    )
    grad_mixed = jnp.concatenate(
        [grad_query.reshape(seq_count, tok_len, features), own_keys, own_values], axis=2
    )
    after = shifted(grad_mixed[:, :2], "ctx", -1)
    extended = jnp.concatenate([grad_mixed, after], axis=1)
    kernel = jnp.concatenate([conv_query, conv_key, conv_value], axis=1).astype(jnp.float32)
    grad_linear = (
        kernel[0] * extended[:, :tok_len]
        + kernel[1] * extended[:, 1 : tok_len + 1]
        + kernel[2] * extended[:, 2:]
    ).astype(jnp.bfloat16)
    grad_kernel = jnp.stack(
        [
            jnp.sum(grad_mixed * padded[:, 2:], axis=(0, 1)),
            jnp.sum(grad_mixed * padded[:, 1 : tok_len + 1], axis=(0, 1)),
            jnp.sum(grad_mixed * padded[:, :tok_len], axis=(0, 1)),
        ]
    )
    grad_lin_rows = grad_linear.reshape(seq_count * tok_len, 3 * features)
    w_joint = jnp.concatenate([w_query, w_key, w_value], axis=1)
    grad_joint = outer_sum(normed_low, grad_lin_rows)
    grad_norm1 = back_prod(grad_lin_rows, w_joint)
    input_part, grad_gattn = norm_back(
        rows_in, factor_attn, gain_attn.astype(jnp.float32), grad_norm1
    )
    input_grad = grad_resid + input_part
    grads = (
        grad_gattn,
        grad_joint[:, :features],
        grad_joint[:, features : 2 * features],
        grad_joint[:, 2 * features :],
        grad_kernel[:, :features],
        grad_kernel[:, features : 2 * features],
        grad_kernel[:, 2 * features :],
        grad_wout,
        grad_bout,
        grad_gffn,
        grad_wup,
        grad_bup,
        grad_wdown,
        grad_bdown,
    )
    return (grads, input_grad)


def general_shards(
    block_input,
    out_grad,
    prefix_len,
    attn_gain,
    q_weight,
    k_weight,
    v_weight,
    conv_q,
    conv_k,
    conv_v,
    out_weight,
    out_bias,
    ffn_gain,
    up_weight,
    up_bias,
    down_weight,
    down_bias,
):
    micro_count = block_input.shape[0]
    local_shape = block_input.shape[1:]
    offset = lax.axis_index("ctx") * block_input.shape[2]
    outputs = []
    input_grads = []
    totals = ()
    for microstep in range(micro_count):
        weights = (
            lax.all_gather(attn_gain, ("dp", "ctx"), axis=0, tiled=True),
            lax.all_gather(q_weight, ("dp", "ctx"), axis=0, tiled=True),
            lax.all_gather(k_weight, ("dp", "ctx"), axis=0, tiled=True),
            lax.all_gather(v_weight, ("dp", "ctx"), axis=0, tiled=True),
            lax.all_gather(conv_q, ("dp", "ctx"), axis=1, tiled=True),
            lax.all_gather(conv_k, ("dp", "ctx"), axis=1, tiled=True),
            lax.all_gather(conv_v, ("dp", "ctx"), axis=1, tiled=True),
            lax.all_gather(out_weight, ("dp", "ctx"), axis=0, tiled=True),
            lax.all_gather(out_bias, ("dp", "ctx"), axis=0, tiled=True),
            lax.all_gather(ffn_gain, ("dp", "ctx"), axis=0, tiled=True),
            lax.all_gather(up_weight, ("dp", "ctx"), axis=0, tiled=True),
            lax.all_gather(up_bias, ("dp", "ctx"), axis=0, tiled=True),
            lax.all_gather(down_weight, ("dp", "ctx"), axis=0, tiled=True),
            lax.all_gather(down_bias, ("dp", "ctx"), axis=0, tiled=True),
        )
        inputs = block_input[microstep].astype(jnp.float32)
        prefix = prefix_len[microstep]
        saved, result = forward_pass(inputs, prefix, weights, offset)
        weights = (
            lax.all_gather(attn_gain, ("dp", "ctx"), axis=0, tiled=True),
            lax.all_gather(q_weight, ("dp", "ctx"), axis=0, tiled=True),
            lax.all_gather(k_weight, ("dp", "ctx"), axis=0, tiled=True),
            lax.all_gather(v_weight, ("dp", "ctx"), axis=0, tiled=True),
            lax.all_gather(conv_q, ("dp", "ctx"), axis=1, tiled=True),
            lax.all_gather(conv_k, ("dp", "ctx"), axis=1, tiled=True),
            lax.all_gather(conv_v, ("dp", "ctx"), axis=1, tiled=True),
            lax.all_gather(out_weight, ("dp", "ctx"), axis=0, tiled=True),
            lax.all_gather(out_bias, ("dp", "ctx"), axis=0, tiled=True),
            lax.all_gather(ffn_gain, ("dp", "ctx"), axis=0, tiled=True),
            lax.all_gather(up_weight, ("dp", "ctx"), axis=0, tiled=True),
            lax.all_gather(up_bias, ("dp", "ctx"), axis=0, tiled=True),
            lax.all_gather(down_weight, ("dp", "ctx"), axis=0, tiled=True),
            lax.all_gather(down_bias, ("dp", "ctx"), axis=0, tiled=True),
        )
        grads, input_grad = backward_pass(saved, out_grad[microstep], prefix, weights, offset)
        totals = (
            grads
            if microstep == 0
            else tuple((earlier + later for earlier, later in zip(totals, grads)))
        )
        outputs.append(result.astype(jnp.bfloat16).reshape(local_shape))
        input_grads.append(input_grad.reshape(local_shape))
    owned = (
        lax.psum_scatter(totals[0], ("dp", "ctx"), scatter_dimension=0, tiled=True),
        lax.psum_scatter(totals[1], ("dp", "ctx"), scatter_dimension=0, tiled=True),
        lax.psum_scatter(totals[2], ("dp", "ctx"), scatter_dimension=0, tiled=True),
        lax.psum_scatter(totals[3], ("dp", "ctx"), scatter_dimension=0, tiled=True),
        lax.psum_scatter(totals[4], ("dp", "ctx"), scatter_dimension=1, tiled=True),
        lax.psum_scatter(totals[5], ("dp", "ctx"), scatter_dimension=1, tiled=True),
        lax.psum_scatter(totals[6], ("dp", "ctx"), scatter_dimension=1, tiled=True),
        lax.psum_scatter(totals[7], ("dp", "ctx"), scatter_dimension=0, tiled=True),
        lax.psum_scatter(totals[8], ("dp", "ctx"), scatter_dimension=0, tiled=True),
        lax.psum_scatter(totals[9], ("dp", "ctx"), scatter_dimension=0, tiled=True),
        lax.psum_scatter(totals[10], ("dp", "ctx"), scatter_dimension=0, tiled=True),
        lax.psum_scatter(totals[11], ("dp", "ctx"), scatter_dimension=0, tiled=True),
        lax.psum_scatter(totals[12], ("dp", "ctx"), scatter_dimension=0, tiled=True),
        lax.psum_scatter(totals[13], ("dp", "ctx"), scatter_dimension=0, tiled=True),
    )
    return (
        jnp.stack(outputs),
        jnp.stack(input_grads),
        owned[0],
        owned[1],
        owned[2],
        owned[3],
        owned[4],
        owned[5],
        owned[6],
        owned[7],
        owned[8],
        owned[9],
        owned[10],
        owned[11],
        owned[12],
        owned[13],
    )


CHIPS = 4
F32 = jnp.float32
BF16 = jnp.bfloat16


def plane_plan(mesh):
    return mesh.shape["ctx"] == 2 * CHIPS and mesh.shape["dp"] == 4


def dot_nn(left, right):
    return jnp.dot(left, right, preferred_element_type=F32)


def dot_nt(left, right):
    return lax.dot_general(left, right, (((1,), (1,)), ((), ())), preferred_element_type=F32)


def dot_tn(left, right):
    return lax.dot_general(left, right, (((0,), (0,)), ((), ())), preferred_element_type=F32)


def call(body, outs, *args, smem=1, hbm=0, scratch=(), name=None, us=0, room=0):
    out_shape = [jax.ShapeDtypeStruct(shape, dtype) for shape, dtype in outs]
    scratch_shapes = [pltpu.VMEM(*spec) if isinstance(spec, tuple) else spec for spec in scratch]
    size = sum(a.size * a.dtype.itemsize for a in args)
    size += sum(int(jnp.dtype(o.dtype).itemsize) * o.size for o in out_shape)
    for spec in scratch:
        if isinstance(spec, tuple):
            size += int(jnp.dtype(spec[1]).itemsize) * functools.reduce(lambda a, b: a * b, spec[0], 1)
    spaces = [pltpu.SMEM] * smem + [pltpu.VMEM] * (len(args) - smem - hbm) + [pltpu.HBM] * hbm
    return pl.pallas_call(
        body,
        out_shape=out_shape,
        compiler_params=pltpu.CompilerParams(vmem_limit_bytes=room or int(size) + (4 << 20)),
        in_specs=[pl.BlockSpec(memory_space=space) for space in spaces],
        out_specs=[pl.BlockSpec(memory_space=pltpu.VMEM)] * len(outs),
        scratch_shapes=scratch_shapes,
        name=name,
        cost_estimate=pl.CostEstimate(flops=1 + us * 10**9, transcendentals=0, bytes_accessed=1),
    )(*args[: len(args) - hbm], *(pltpu.with_memory_space_constraint(a, pltpu.HBM) for a in args[len(args) - hbm :]))


def send(value, bits):
    dp, ctx = lax.axis_size("dp"), lax.axis_size("ctx")
    pairs = [(i, (i // ctx) * ctx + ((i % ctx) ^ bits)) for i in range(dp * ctx)]
    return lax.ppermute(value, ("dp", "ctx"), pairs)


def send_z(value, bits):
    dp, ctx = lax.axis_size("dp"), lax.axis_size("ctx")
    pairs = [(i, ((i // ctx) ^ bits) * ctx + i % ctx) for i in range(dp * ctx)]
    return lax.ppermute(value, ("dp", "ctx"), pairs)


def after(value, *waits):
    return lax.optimization_barrier((value, *waits))[0]


def all_after(values, *waits):
    return list(lax.optimization_barrier((*values, *waits))[: len(values)])


def to_chips(blocks):
    return [blocks[0]] + [send(blocks[j], 2 * j) for j in range(1, CHIPS)]


def stack_k(ids, s0, s1, s2, s3, out):
    for r, ref in enumerate((s0, s1, s2, s3)):
        out[r] = ref[...]


def join_k(ids, mine, other, keep, later, now):
    n = keep.shape[0]
    for r, out in ((0, keep), (2, later), (1, now.at[0]), (3, now.at[1])):
        at = slice(r * n, r * n + n)
        out[...] = (mine[at].astype(F32) + other[at].astype(F32)).astype(BF16)


def pass_on_k(ids, later, got, out):
    out[...] = (later[...].astype(F32) + got[1].astype(F32)).astype(BF16)


def join_cores(ids, keep, away, name):
    size = (keep.shape[0] // 4, *keep.shape[1:])
    return call(
        join_k, [(size, BF16)] * 2 + [((2, *size), BF16)], ids, keep, away, name="join_" + name
    )


def to_all_chips(block):
    half = block.shape[0] // 2
    one, two = send(block, 2), send(block, 4)
    return [block, one, two, send(one[:half], 4), send(two[half:], 2)]


def add_half_k(ids, one, two, low, high, one_out, two_out):
    half = low.shape[0]
    one_out[:half, :] = one[:half, :]
    one_out[half:, :] = (one[half:, :].astype(F32) + high[...].astype(F32)).astype(BF16)
    two_out[half:, :] = two[half:, :]
    two_out[:half, :] = (two[:half, :].astype(F32) + low[...].astype(F32)).astype(BF16)


def to_owners(ids, own, one, two, low, high, *first):
    low, high = all_after([send(low, 2), send(high, 4)], *first)
    one, two = call(add_half_k, [(one.shape, BF16)] * 2, ids, one, two, low, high, name="add_half")
    return own, one, two


ROWS = ((0, 256), (256, 512), (512, 768), (768, 896), (896, 1024))


def place_k(ids, other, mine, out, sem):
    c = ids[2]
    rows = other.shape[2]
    copy = pltpu.make_async_copy(mine.at[c, 0], out.at[pl.ds(pl.multiple_of(c * rows, rows), rows), :], sem)
    copy.start()
    out[pl.ds(pl.multiple_of((1 - c) * rows, rows), rows), :] = other[c, 0]
    copy.wait()


def pack_k(ids, *refs):
    k = ids[1]
    args, (p0, p1, p2, p3), stage, held, sems = refs[:13], refs[13:17], refs[17], refs[18:31], refs[31]
    copies = [pltpu.make_async_copy(ref, to, sems.at[i]) for i, (ref, to) in enumerate(zip(args, held))]
    for copy in copies:
        copy.start()
    for copy in copies:
        copy.wait()
    wq, wk, wv, up, wo, *vectors, bias_u = held
    rows = jnp.concatenate([ref[...].astype(F32).reshape(-1, 24) for ref in vectors], axis=0)
    rows = jnp.concatenate([rows, jnp.zeros((128 - rows.shape[0], 24), F32)], axis=0)
    rows = jnp.concatenate([rows, jnp.zeros((128, 104), F32)], axis=1)
    cols = rows.T[:24, :16]
    bias = bias_u[...].astype(F32).reshape(1, 96)
    bias = jnp.concatenate([bias[:, 24 * i : 24 * i + 24] for i in range(4)] + [jnp.zeros((20, 24), F32)], axis=0)
    tail = jnp.concatenate([cols, bias, jnp.zeros((24, 24), F32)], axis=1).astype(BF16)
    for chip in range(CHIPS):
        lo = 192 * chip
        for part, ref in enumerate((wq, wk, wv)):
            stage[chip, :, 192 * part : 192 * part + 192] = ref[:, lo : lo + 192]
        stage[chip, :, 576:640] = tail
        for plane in range(4):
            at = 640 + 192 * plane
            stage[chip, :, at : at + 192] = up[:, 768 * plane + lo : 768 * plane + lo + 192]
        stage[chip, :, 1408:2176] = wo[...]
    for j, out in enumerate((p0, p1, p2, p3)):
        out[...] = stage[k ^ j]


def split_k(ids, p0, p1, p2, p3, a_out, b_out):
    for j, ref in enumerate((p0, p1, p2, p3)):
        a_out[j] = ref[:, :640]
        b_out[j] = ref[:, 640:1408]
        b_out[CHIPS + j] = ref[:, 1408:2176]


def with_down_k(ids, b, wd, b_out, sems):
    n = b.shape[0]
    copies = [
        pltpu.make_async_copy(wd.at[24 * j : 24 * j + 24, :], b_out.at[n + j], sems.at[j]) for j in range(CHIPS)
    ]
    for copy in copies:
        copy.start()
    b_out[0:n] = b[...]
    for copy in copies:
        copy.wait()


def gather_b_k(ids, mine, other, up_out, wo_out, wd_out):
    z, k, c = ids[0], ids[1], ids[2]
    for core, ref in enumerate((mine, other)):
        for plane in range(4):
            for j in range(CHIPS):
                at = (z ^ plane) * 8 + (k ^ j) * 2 + (c ^ core)
                up_out[at] = ref[plane, j]
                wo_out[at] = ref[plane, CHIPS + j]
                wd_out[((z ^ plane) * 2 + (c ^ core)) * 4 + j] = ref[plane, 8 + j]


def hidden_grad_k(ids, g0, g1, g2, g3, g4, wd, dh, g_all):
    for ref, (lo, hi) in zip((g0, g1, g2, g3, g4), ROWS):
        g_all[lo:hi, :] = ref[...]

    dh[...] = dot_nt(g_all[...], wd[...]).astype(BF16)


def mask_rows(b, prefix, out):
    cols = max(256 * (b + 1), 512)
    row_ids = 256 * b + lax.broadcasted_iota(jnp.int32, (256, cols), 0)
    col_ids = lax.broadcasted_iota(jnp.int32, (256, cols), 1)
    out[:, :cols] = jnp.where((col_ids <= row_ids) | (col_ids < prefix), 0.0, NEG)
    return cols


def attend_k(
    ids, pre, *refs,
):
    n_x = len(refs) - 21
    pieces, xs, refs = refs[:2], refs[2 : 2 + n_x], refs[2 + n_x :]
    w_out, bias_out, a_out, lin, q_out, k_out, v_out, o0, o1, o2, o3, att, lse, small_out, kern_out = refs[:15]
    w_scr, stage, mask, mixed = refs[15:]
    z, k, c = ids[0], ids[1], ids[2]
    prefix = pre[c, 0]
    for core in range(2):
        for plane in range(4):
            for j in range(CHIPS):
                w_scr[(z ^ plane) * 8 + (k ^ j) * 2 + (c ^ core)] = pieces[core][plane, j].astype(F32)
    bias_out[...] = jnp.zeros_like(bias_out)
    for plane in range(4):
        for core in range(2):
            piece = w_scr[plane * 8 + k * 2 + core, :, 512:640]
            for part in range(4):
                at = 96 * (2 * plane + core) + 24 * part
                bias_out[0:1, at : at + 24] = piece[part : part + 1, 80:104]
    small = w_scr[:, :, 512:640].reshape(768, 128).T[64:80]
    w_out[...] = w_scr[:, :, 0:576].reshape(768, 576).astype(BF16)
    small_out[...] = small
    gain = small[0:1]
    own = jnp.zeros((9, 192), F32)
    for chip in range(CHIPS):
        own = jnp.where(k == chip, small[1:10, 192 * chip : 192 * chip + 192], own)
    kern = jnp.concatenate([own[0:3], own[3:6], own[6:9]], axis=1)
    kern_out[...] = kern
    lin[0:8, :] = jnp.zeros((8, lin.shape[1]), F32)
    for ref, (lo, hi) in zip(xs, ROWS if n_x == 5 else ROWS[:3] + ((768, 1024),)):
        at = pl.multiple_of((k ^ (lo // 256)) * 256 + lo % 256, 128)
        x = ref[...].astype(F32)
        factor = lax.rsqrt(jnp.mean(x * x, axis=-1, keepdims=True) + EPS)
        a_out[pl.ds(at, hi - lo), :] = (x * factor * gain).astype(BF16)

    lin[8:1032, :] = dot_nn(a_out[...], w_out[...])
    for b in range(4):
        t = 256 * b
        mixed[...] = (
            kern[0:1] * lin[8 + t : 264 + t, :]
            + kern[1:2] * lin[7 + t : 263 + t, :]
            + kern[2:3] * lin[6 + t : 262 + t, :]
        ).astype(BF16)
        for h in range(3):
            lo = 64 * h
            q_out[h, t : t + 256, :] = mixed[:, lo : lo + 64] * BF16(HEAD ** (-0.5))
            k_out[h, t : t + 256, :] = mixed[:, 192 + lo : 256 + lo]
            v_out[h, t : t + 256, :] = mixed[:, 384 + lo : 448 + lo]
    for b in range(4):
        t = 256 * b
        cols = mask_rows(b, prefix, mask)

        for h in range(3):
            scores = dot_nt(q_out[h, t : t + 256, :], k_out[h, 0:cols, :]) + mask[:, :cols]
            top = jnp.max(scores, axis=-1, keepdims=True)
            weight = jnp.exp(scores - top)
            total = jnp.sum(weight, axis=-1, keepdims=True)
            att[h, t : t + 256, :] = dot_nn(weight.astype(BF16), v_out[h, 0:cols, :]) * (1.0 / total)
            lse[h, t : t + 256, :] = top + jnp.log(total)
        stage[b] = jnp.concatenate([att[h, t : t + 256, :] for h in range(3)], axis=1).astype(BF16)
    for j, out in enumerate((o0, o1, o2, o3)):
        out[...] = stage[k ^ j]


def resid_k(ids, t0, t1, t2, t3, wo, xw, small, x1_out, a2_out):
    k = ids[1]
    total = xw[...].astype(F32) + small[10:11]
    for j, ref in enumerate((t0, t1, t2, t3)):
        at = pl.multiple_of((k ^ j) * 192, 192)
        total = total + dot_nn(ref[...], wo[pl.ds(at, 192), :])
    x1_out[...] = total
    factor = lax.rsqrt(jnp.mean(total * total, axis=-1, keepdims=True) + EPS)
    a2_out[...] = (total * factor * small[11:12]).astype(BF16)


def ffn_k(ids, *refs):
    n_a = len(refs) - 12
    blocks, refs = refs[:n_a], refs[n_a:]
    dh, up, bias, hsq, du, a_all, p0, p1, p2, p3, p4, stage = refs
    for ref, (lo, hi) in zip(blocks, ROWS if n_a == 5 else ROWS[:3] + ((768, 1024),)):
        a_all[lo:hi, :] = ref[...]

    act = jax.nn.relu(dot_nn(a_all[...], up[...]) + bias[...])
    hsq[...] = (act * act).astype(BF16)
    du[...] = (dh[...].astype(F32) * 2.0 * act).astype(BF16)
    stage[...] = dot_nt(du[...], up[...]).astype(BF16)
    for ref, (lo, hi) in zip((p0, p1, p2, p3, p4), ROWS):
        ref[...] = stage[lo:hi, :]


def ffn_out_k(ids, hsq, wd, p0, p1, p2, p3):
    for j, out in enumerate((p0, p1, p2, p3)):
        out[...] = dot_nn(hsq[256 * j : 256 * j + 256, :], wd[...]).astype(BF16)


def ffn_grads_k(ids, a_all, g_all, hsq, du, keep, away, bias_out, stage):
    z, k, c = ids[0], ids[1], ids[2]
    bias_out[...] = jnp.sum(du[...].astype(F32), axis=0, keepdims=True)
    up_grad = dot_tn(a_all[...], du[...])
    for plane in range(4):
        for core in range(2):
            to, at = c ^ core, (z ^ plane) * 8
            for chip in range(CHIPS):
                row = 24 * (plane * 8 + chip * 2 + core)
                stage[to, at + (k ^ chip)] = up_grad[row : row + 24].astype(BF16)
    down_grad = dot_tn(hsq[...], g_all[...])
    for plane in range(4):
        for core in range(2):
            to, at = c ^ core, (z ^ plane) * 8
            for chip in range(CHIPS):
                row = 96 * (plane * 2 + core) + 24 * chip
                stage[to, at + 4 + chip] = down_grad[row : row + 24].astype(BF16)
    keep[...] = stage[0]
    away[...] = stage[1]


def sum_planes_k(ids, *refs):
    f, o, r, (d_out, *outs) = refs[0:3], refs[3:6], refs[6:9], refs[9:]

    def total(parts, at):
        return parts[0][at].astype(F32) + parts[1][0, at].astype(F32) + parts[2][at].astype(F32)

    for j, out in enumerate(outs):
        out[:, 0:640] = total(r, j).astype(BF16)
        out[:, 640:1408] = total(f, j).astype(BF16)
        out[:, 1408:2176] = total(o, j).astype(BF16)
        d_out[24 * j : 24 * j + 24, :] = total(f, CHIPS + j)


def mid_grad_k(
    ids, p0, p1, p2, x1, gw, small, wo, dx_out, dz_out, bias_out, o0, o1, o2, o3
):
    k = ids[1]
    da2 = p0[...].astype(F32) + p1[...].astype(F32) + p2[...].astype(F32)
    val = x1[...]
    factor = lax.rsqrt(jnp.mean(val * val, axis=-1, keepdims=True) + EPS)
    weighted = da2 * small[11:12]
    inner = jnp.mean(weighted * val, axis=-1, keepdims=True)
    dx = gw[...].astype(F32) + factor * weighted - val * (factor * factor * factor * inner)
    dx_out[...] = dx
    low = dx.astype(BF16)
    dz_out[...] = low
    bias_out[...] = jnp.sum(low.astype(F32), axis=0, keepdims=True)
    for j, out in enumerate((o0, o1, o2, o3)):
        at = pl.multiple_of((k ^ j) * 192, 192)
        out[...] = dot_nt(low, wo[pl.ds(at, 192), :]).astype(BF16)


def out_grads_k(ids, t0, t1, t2, t3, dz, keep, away, stage):
    z, k, c = ids[0], ids[1], ids[2]
    for j, ref in enumerate((t0, t1, t2, t3)):
        part = dot_tn(ref[...], dz[...])
        at = ((k ^ j) ^ z) * 4
        for chip in range(CHIPS):
            for core in range(2):
                row = 24 * (2 * chip + core)
                stage[c ^ core, at + (k ^ chip)] = part[row : row + 24].astype(BF16)
    keep[...] = stage[0]
    away[...] = stage[1]


def attend_grad_k(
    ids, pre, d0, d1, d2, d3, q_in, k_in, v_in, att, lse, lin, kern, w,
    dlin_out, conv_out, p0, p1, p2, p3, p4, do_scr, dm, mask, dq, dk, dv, stage,
):
    k, c = ids[1], ids[2]
    prefix = pre[c, 0]
    for j, ref in enumerate((d0, d1, d2, d3)):
        for h in range(3):
            do_scr[h, pl.ds(pl.multiple_of((k ^ j) * 256, 256), 256), :] = ref[:, 64 * h : 64 * h + 64]
    dm[1024:1032, :] = jnp.zeros((8, 576), F32)
    for b in (3, 2, 1, 0):
        t = 256 * b
        cols = mask_rows(b, prefix, mask)

        for h in range(3):
            q_rows, do_rows = q_in[h, t : t + 256, :], do_scr[h, t : t + 256, :]
            scores = dot_nt(q_rows, k_in[h, 0:cols, :]) + mask[:, :cols]
            probs = jnp.exp(scores - lse[h, t : t + 256, :])
            delta = jnp.sum(do_rows.astype(F32) * att[h, t : t + 256, :], axis=-1, keepdims=True)
            dprobs = dot_nt(do_rows, v_in[h, 0:cols, :])
            dscores = (probs * (dprobs - delta)).astype(BF16)
            dq[h, t : t + 256, :] = dot_nn(dscores, k_in[h, 0:cols, :]) * HEAD ** (-0.5)
            dk_part = dot_tn(q_rows, dscores)
            dv_part = dot_tn(do_rows, probs.astype(BF16))
            if b == 3:
                dk[h] = dk_part
                dv[h] = dv_part
            else:
                dk[h, :, 0:cols] = dk[h, :, 0:cols] + dk_part
                dv[h, :, 0:cols] = dv[h, :, 0:cols] + dv_part
    for h in range(3):
        dm[0:1024, 64 * h : 64 * h + 64] = dq[h]
        dm[0:1024, 192 + 64 * h : 256 + 64 * h] = dk[h].T
        dm[0:1024, 384 + 64 * h : 448 + 64 * h] = dv[h].T
    taps = kern[...]
    sums = [jnp.zeros((1, 576), F32) for _ in range(3)]
    for b in range(4):
        t = 256 * b
        here = dm[t : t + 256, :]
        dlin_out[t : t + 256, :] = (
            taps[0:1] * here + taps[1:2] * dm[t + 1 : t + 257, :] + taps[2:3] * dm[t + 2 : t + 258, :]
        ).astype(BF16)
        for back in range(3):
            sums[back] = sums[back] + jnp.sum(
                here * lin[8 - back + t : 264 - back + t, :], axis=0, keepdims=True
            )
    conv_out[...] = jnp.concatenate(sums, axis=0)

    stage[...] = dot_nt(dlin_out[...], w[...]).astype(BF16)
    for ref, (lo, hi) in zip((p0, p1, p2, p3, p4), ROWS):
        at = pl.multiple_of((k ^ (lo // 256)) * 256 + lo % 256, 128)
        ref[...] = stage[pl.ds(at, hi - lo), :]


def proj_grads_k(ids, a1, dlin, conv, up_bias, out_bias, g, keep, away, stage):
    z, k, c = ids[0], ids[1], ids[2]
    grad = dot_tn(a1[...], dlin[...])
    conv_rows = jnp.concatenate([conv[:, 0:192], conv[:, 192:384], conv[:, 384:576]], axis=0)
    conv_all = jnp.concatenate(
        [jnp.where(k == chip, conv_rows, 0.0) for chip in range(CHIPS)], axis=1
    )
    down_bias = jnp.sum(g[...].astype(F32), axis=0, keepdims=True)
    rows = jnp.concatenate(
        [conv_all, out_bias[...], down_bias, jnp.zeros((117, 768), F32)], axis=0
    )
    cols = rows.T
    for plane in range(4):
        for chip in range(CHIPS):
            for core in range(2):
                row = 24 * (plane * 8 + chip * 2 + core)
                to, at = c ^ core, (z ^ plane) * 4 + (k ^ chip)
                stage[to, at, :, 0:576] = grad[row : row + 24]
                stage[to, at, :, 576:640] = cols[row : row + 24, 0:64]
    for plane in range(4):
        for core in range(2):
            for part in range(4):
                lo = 96 * (2 * plane + core) + 24 * part
                stage[c ^ core, (z ^ plane) * 4, part : part + 1, 592:616] = up_bias[0:1, lo : lo + 24]
    keep[...] = stage[0].astype(BF16)
    away[...] = stage[1].astype(BF16)


def halves_k(ids, total_fn, keep, away):
    c = ids[2]
    keep[...] = total_fn(pl.ds(pl.multiple_of(c * 128, 128), 128)).astype(keep.dtype)
    away[...] = total_fn(pl.ds(pl.multiple_of((1 - c) * 128, 128), 128)).astype(away.dtype)


def output_k(ids, p0, p1, p2, p3, x1, small, keep, away):
    def rows_of(at):
        total = p0[at, :].astype(F32) + p1[at, :].astype(F32) + p2[at, :].astype(F32)
        return x1[at, :] + (total + p3[at, :].astype(F32)) + small[12:13]

    halves_k(ids, rows_of, keep, away)


def input_grad_k(ids, p0, p1, p2, xw, dx, small, keep, away):
    def rows_of(at):
        da1 = p0[at, :].astype(F32) + p1[at, :].astype(F32) + p2[at, :].astype(F32)
        val = xw[at, :].astype(F32)
        factor = lax.rsqrt(jnp.mean(val * val, axis=-1, keepdims=True) + EPS)
        weighted = da1 * small[0:1]
        inner = jnp.mean(weighted * val, axis=-1, keepdims=True)
        return dx[at, :] + factor * weighted - val * (factor * factor * factor * inner)

    halves_k(ids, rows_of, keep, away)


def deliver_k(ids, out_keep, out_recv, in_keep, in_recv, out_ref, in_ref):
    c = ids[2]
    out_ref[c, 0] = out_keep[...]
    out_ref[1 - c, 0] = out_recv[...]
    in_ref[c, 0] = in_keep[...]
    in_ref[1 - c, 0] = in_recv[...]


def owned_k(
    ids, s0, s1, s2, s3, wq, wk, wv, up, gain_a, gain_f,
    gq, gk, gv, cq, ck, cv, go, gu, ga, gf, bo, bd, bu, stage_r, stage_u,
):
    k = ids[1]
    extra = jnp.zeros((24, 128), F32)
    out_sum = jnp.zeros((24, 768), F32)
    for j, ref in enumerate((s0, s1, s2, s3)):
        stage_r[k ^ j] = ref[:, 0:640].astype(F32)
        stage_u[k ^ j] = ref[:, 640:1408].astype(F32)
        out_sum = out_sum + ref[:, 1408:2176].astype(F32)
        extra = extra + ref[:, 512:640].astype(F32)
    go[...] = out_sum
    for chip in range(CHIPS):
        lo = 192 * chip
        for part, ref in enumerate((gq, gk, gv)):
            ref[:, lo : lo + 192] = stage_r[chip, :, 192 * part : 192 * part + 192]
        for plane in range(4):
            at = 768 * plane + lo
            gu[:, at : at + 192] = stage_u[chip, :, 192 * plane : 192 * plane + 192]
    attn = jnp.sum(
        gq[...] * wq[...].astype(F32) + gk[...] * wk[...].astype(F32) + gv[...] * wv[...].astype(F32),
        axis=-1, keepdims=True,
    )
    ffn = jnp.sum(gu[...] * up[...].astype(F32), axis=-1, keepdims=True)
    cols = jnp.concatenate([extra[:, 64:75], attn, ffn, jnp.zeros((24, 115), F32)], axis=1)
    cols = jnp.concatenate([cols, jnp.zeros((104, 128), F32)], axis=0)
    rows = cols.T[:16, :24]
    for at, ref in ((0, cq), (3, ck), (6, cv)):
        ref[...] = rows[at : at + 3]
    bo[...] = rows[9]
    bd[...] = rows[10]
    ga[...] = rows[11] / gain_a[...].astype(F32)
    gf[...] = rows[12] / gain_f[...].astype(F32)
    bu[...] = jnp.concatenate([extra[i : i + 1, 80:104] for i in range(4)], axis=1).reshape(96)


def plane_shards(block_input, out_grad, prefix_len, attn_gain, q_weight, k_weight, v_weight, conv_q, conv_k, conv_v, out_weight, out_bias, ffn_gain, up_weight, up_bias, down_weight, down_bias):
    z, place = (lax.axis_index('dp'), lax.axis_index('ctx'))
    ids = jnp.stack([z, place // 2, place % 2]).astype(jnp.int32)
    block, half = (((256, 768), BF16), ((128, 768), BF16))
    blocks = [block] * 3 + [half] * 2
    tall, heads = (((1024, 768), BF16), (3, 1024, 64))
    rows = (128, 768)
    sem = pltpu.SemaphoreType.DMA
    x_peer = send(block_input, 1)
    weights = (q_weight, k_weight, v_weight, up_weight, out_weight, attn_gain, conv_q, conv_k, conv_v, out_bias, ffn_gain, down_bias, up_bias)
    packs = call(pack_k, [((24, 2176), BF16)] * 4, ids, *weights, hbm=13, scratch=[((4, 24, 2176), BF16)] + [(w.shape, BF16) for w in weights] + [sem((13,))], name='pack')
    packs = to_chips(packs)
    x_peer = after(x_peer, *packs[1:2])
    xw, = call(place_k, [block], ids, x_peer, block_input, hbm=1, scratch=[sem(())], name='place_x')
    x_one, x_two = (send(xw, 2), send(xw, 4))
    a_own, b_own = call(split_k, [((4, 24, 640), BF16), ((8, 24, 768), BF16)], ids, *packs, name='split')
    a_two, a_one = (send_z(a_own, 2), send_z(a_own, 1))
    a_three = send_z(a_own, 3)
    x_low, x_high = (send(part, bits) for part, bits in zip(all_after([x_one[:128], x_two[128:]], a_two), (4, 2)))
    xs = [xw, x_one, x_two, x_low, x_high]
    bdep = ()
    b_own, = call(with_down_k, [((12, 24, 768), BF16)], ids, after(b_own, *bdep), down_weight, hbm=1, scratch=[sem((4,))], name='with_down')
    wd_dep = b_own
    g_peer = send(after(out_grad, *packs[1:]), 1)
    gw, = call(place_k, [block], ids, g_peer, out_grad, hbm=1, scratch=[sem(())], name='place_g')
    a_last = after(a_three, wd_dep)
    a_all, = call(stack_k, [((4, 4, 24, 640), BF16)], ids, a_own, a_one, a_two, a_last, name='stack_a')
    a_peer = send(a_all, 1)
    b_own = after(b_own, a_three)
    b_one, b_two = (send_z(b_own, 1), send_z(b_own, 2))
    gsrc = after(gw, *xs[1:3])
    g_one, g_two = (send(gsrc, 2), send(gsrc, 4))
    w_a, up_bias_row, a1, lin, q, k, v, t0, t1, t2, t3, att, lse, small, kern = call(attend_k, [((768, 576), BF16), ((1, 768), F32), tall, ((1032, 576), F32)] + [(heads, BF16)] * 3 + [((256, 192), BF16)] * 4 + [(heads, F32), ((3, 1024, 1), F32), ((16, 768), F32), ((3, 576), F32)], ids, prefix_len, after(a_all, gw), a_peer, *xs, smem=2, name='attend', scratch=[((32, 24, 640), F32), ((4, 256, 192), BF16), ((256, 1024), F32), ((256, 576), BF16)])
    atts = [t0, send(t1, 2), send(t2, 4)]
    atts.append(send(after(t3, *atts[1:2]), 6))
    g_one, g_two = all_after([g_one, g_two], t1)
    g_low, g_high = (send(part, bits) for part, bits in zip([g_one[:128], g_two[128:]], (4, 2)))
    sdep = [*atts[1:3], *(g_low, g_high)]
    b_one, b_two = all_after([b_one, b_two], t1)
    b_three = send_z(b_two, 1)
    b_all, = call(stack_k, [((4, 12, 24, 768), BF16)], ids, b_own, *all_after([b_one, b_two, b_three], *sdep), name='stack_b')
    w_up, w_o, w_d = [w.reshape(768, 768) for w in call(gather_b_k, [((32, 24, 768), BF16)] * 3, ids, b_all, send(b_all, 1), name='gather_b')]
    x1, a2 = call(resid_k, [((256, 768), F32), block], ids, *atts, w_o, xw, small, name='resid')
    a2s = to_all_chips(a2)
    dh, g_all = call(hidden_grad_k, [tall] * 2, ids, gw, g_one, g_two, g_low, g_high, w_d, name='hidden_grad')
    hsq, du, a2_all, *da2 = call(ffn_k, [tall] * 3 + blocks, ids, *a2s, dh, w_up, up_bias_row, scratch=[tall], name='ffn')
    da2_parts = da2
    f_keep, f_away, up_bias_grad = call(ffn_grads_k, [((32, 24, 768), BF16)] * 2 + [((1, 768), F32)], ids, a2_all, g_all, hsq, du, scratch=[((2, 32, 24, 768), BF16)], name='ffn_grads', us=1000)
    d_first = []
    d_first.append(up_bias_grad)
    da2, da2_one, da2_two = to_owners(ids, *da2_parts, *d_first)
    da2 = [da2, send(da2_one, 2), send(da2_two, 4)]
    mid_first = []
    outs = list(call(ffn_out_k, [block] * 4, ids, hsq, after(w_d, da2_one), name='ffn_out'))
    mid_first.append(outs[0])
    f_peer = send(after(f_away, da2_one), 1)
    f_keep, f_later, f_now = join_cores(ids, f_keep, f_peer, 'f')
    f_now = send_z(f_now, 1)
    mid_first.append(f_keep)
    dx, dz, out_bias_grad, *datt = call(mid_grad_k, [((256, 768), F32), block, ((1, 768), F32)] + [((256, 192), BF16)] * 4, ids, *da2, x1, after(gw, *mid_first), small, w_o, name='mid_grad')
    datt = to_chips(datt)
    ag_first = []
    o_keep, o_away = call(out_grads_k, [((16, 24, 768), BF16)] * 2, ids, *atts, dz, scratch=[((2, 16, 24, 768), BF16)], name='out_grads')
    ag_first.append(o_keep)
    pj_first = []
    f_now = after(f_now, *datt[1:])
    f_later, = call(pass_on_k, [(f_later.shape, BF16)], ids, f_later, f_now, name='pass_f')
    f_sent = send_z(f_later, 2)
    ag_first.append(f_later)
    pj_first.append(f_sent)
    outs[1:] = all_after(outs[1:], *datt[1:])
    outs[1], outs[2] = (send(outs[1], 2), send(outs[2], 4))
    pj_first += outs[1:3]
    dlin, conv_grad, *da1 = call(attend_grad_k, [((1024, 576), BF16), ((3, 576), F32)] + blocks, ids, prefix_len, *datt, after(q, *ag_first), k, v, att, lse, lin, kern, w_a, smem=2, name='attend_grad', scratch=[(heads, BF16), ((1032, 576), F32), ((256, 1024), F32), (heads, F32)] + [((3, 64, 1024), F32)] * 2 + [tall])
    o_peer = send(after(o_away, dlin), 1)
    r_keep, r_away = call(proj_grads_k, [((16, 24, 640), BF16)] * 2, ids, after(a1, *pj_first), dlin, conv_grad, up_bias_grad, out_bias_grad, gw, scratch=[((2, 16, 24, 640), F32)], name='proj_grads')
    r_peer = send(r_away, 1)
    r_keep, r_later, r_now = join_cores(ids, r_keep, r_peer, 'r')
    r_now = send_z(r_now, 1)
    o_keep, o_later, o_now = join_cores(ids, o_keep, o_peer, 'o')
    o_now = send_z(o_now, 1)
    o_now = after(o_now, r_keep)
    o_later, = call(pass_on_k, [(o_later.shape, BF16)], ids, o_later, o_now, name='pass_o')
    o_sent = send_z(o_later, 2)
    da1, da1_one, da1_two = to_owners(ids, *da1)
    r_later, = call(pass_on_k, [(r_later.shape, BF16)], ids, r_later, r_now, name='pass_r')
    da1 = [da1, send(da1_one, 2), send(da1_two, 4)]
    r_sent = send_z(r_later, 2)
    outs[3] = send(after(outs[3], r_keep), 6)
    out_keep, out_away = call(output_k, [(rows, BF16)] * 2, ids, *outs, after(x1, r_later), small, name='output')
    out_recv = send(out_away, 1)
    in_keep, in_away = call(input_grad_k, [(rows, F32)] * 2, ids, *da1, xw, dx, small, name='input_grad')
    in_recv = send(in_away, 1)
    o_parts = [o_keep, o_now, o_sent]
    f_parts = [f_keep, f_now, f_sent]
    r_parts = [r_keep, r_now, r_sent]
    down_grad, *sums = call(sum_planes_k, [((96, 768), F32)] + [((24, 2176), BF16)] * 4, ids, *f_parts, *o_parts, *r_parts, name='sum_planes')
    sums = to_chips(sums)
    block_output, input_grad = call(deliver_k, [((2, 1, 128, 768), BF16), ((2, 1, 128, 768), F32)], ids, out_keep, out_recv, in_keep, in_recv, name='deliver', us=100)
    vec = ((24,), F32)
    gq, gk, gv, cq, ck, cv, go, gu, ga, gf, bo, bd, bu = call(owned_k, [((24, 768), F32)] * 3 + [((3, 24), F32)] * 3 + [((24, 768), F32), ((24, 3072), F32)] + [vec] * 4 + [((96,), F32)], ids, sums[0], *sums[1:], q_weight, k_weight, v_weight, up_weight, attn_gain, ffn_gain, scratch=[((4, 24, 640), F32), ((4, 24, 768), F32)], name='owned', us=100)
    return (block_output, input_grad, ga, gq, gk, gv, cq, ck, cv, go, bo, gf, gu, bu, down_grad, bd)


def solution(mesh):
    plan = plane_shards if plane_plan(mesh) else general_shards
    in_specs = (
        P(None, "dp", "ctx", None),
        P(None, "dp", "ctx", None),
        P(None, "dp"),
        P(("dp", "ctx")),
        P(("dp", "ctx"), None),
        P(("dp", "ctx"), None),
        P(("dp", "ctx"), None),
        P(None, ("dp", "ctx")),
        P(None, ("dp", "ctx")),
        P(None, ("dp", "ctx")),
        P(("dp", "ctx"), None),
        P(("dp", "ctx")),
        P(("dp", "ctx")),
        P(("dp", "ctx"), None),
        P(("dp", "ctx")),
        P(("dp", "ctx"), None),
        P(("dp", "ctx")),
    )
    out_specs = (
        P(None, "dp", "ctx", None),
        P(None, "dp", "ctx", None),
        P(("dp", "ctx")),
        P(("dp", "ctx"), None),
        P(("dp", "ctx"), None),
        P(("dp", "ctx"), None),
        P(None, ("dp", "ctx")),
        P(None, ("dp", "ctx")),
        P(None, ("dp", "ctx")),
        P(("dp", "ctx"), None),
        P(("dp", "ctx")),
        P(("dp", "ctx")),
        P(("dp", "ctx"), None),
        P(("dp", "ctx")),
        P(("dp", "ctx"), None),
        P(("dp", "ctx")),
    )
    return jax.shard_map(plan, mesh=mesh, in_specs=in_specs, out_specs=out_specs, check_vma=False)
```

```python
import functools

import jax
import jax.numpy as jnp
from jax import lax
from jax.experimental import pallas as pl
from jax.experimental.pallas import tpu as pltpu
from jax.sharding import PartitionSpec as P

HEADS = 12
HEAD = 64


EPS = 1e-06
NEG = -1e30


def shifted(shard, axis, by):
    peers = lax.axis_size(axis)
    pairs = [(i, i + by) for i in range(peers) if 0 <= i + by < peers]
    return lax.ppermute(shard, axis, pairs)


def norm_rows(values, gain_vec):
    factor = lax.rsqrt(jnp.mean(values * values, axis=-1, keepdims=True) + EPS)
    return (factor, values * factor * gain_vec)


def norm_back(values, factor, gain_vec, grad_out):
    weighted = grad_out * gain_vec
    inner = jnp.mean(weighted * values, axis=-1, keepdims=True)
    return (
        factor * weighted - values * factor**3 * inner,
        jnp.sum(grad_out * values * factor, axis=0),
    )


def outer_sum(left, right):
    return lax.dot_general(
        left, right, (((0,), (0,)), ((), ())), preferred_element_type=jnp.float32
    )


def back_prod(grad_rows, weight):
    return lax.dot_general(
        grad_rows, weight, (((1,), (1,)), ((), ())), preferred_element_type=jnp.float32
    )


def scores_of(query, key_part, key_start, offset, prefix):
    raw_scores = jnp.einsum("sthe,skhe->shtk", query, key_part, preferred_element_type=jnp.float32)
    row_ids = offset + jnp.arange(query.shape[1], dtype=jnp.int32)
    col_ids = key_start + jnp.arange(key_part.shape[1], dtype=jnp.int32)
    allowed = (col_ids[None, None, :] <= row_ids[None, :, None]) | (
        col_ids[None, None, :] < prefix[:, None, None]
    )
    return jnp.where(allowed[:, None], raw_scores * HEAD ** (-0.5), NEG)


def forward_pass(inputs, prefix, weights, offset):
    (
        gain_attn,
        w_query,
        w_key,
        w_value,
        conv_query,
        conv_key,
        conv_value,
        w_out,
        b_out,
        gain_ffn,
        w_up,
        b_up,
        w_down,
        b_down,
    ) = weights
    seq_count, tok_len, features = inputs.shape
    length = tok_len * lax.axis_size("ctx")
    key_block = min(512, length)
    block_count = length // key_block
    rows_in = inputs.reshape(seq_count * tok_len, features)
    factor_attn, normed = norm_rows(rows_in, gain_attn.astype(jnp.float32))
    normed_low = normed.astype(jnp.bfloat16)
    w_joint = jnp.concatenate([w_query, w_key, w_value], axis=1)
    kernel = jnp.concatenate([conv_query, conv_key, conv_value], axis=1).astype(jnp.float32)
    linear = jnp.dot(normed_low, w_joint, preferred_element_type=jnp.float32).reshape(
        seq_count, tok_len, 3 * features
    )
    before = shifted(linear[:, tok_len - 2 :], "ctx", 1)
    padded = jnp.concatenate([before, linear], axis=1)
    mixed = (
        kernel[0] * padded[:, 2:]
        + kernel[1] * padded[:, 1 : tok_len + 1]
        + kernel[2] * padded[:, :tok_len]
    ).astype(jnp.bfloat16)
    query = mixed[:, :, :features].reshape(seq_count, tok_len, HEADS, HEAD)
    keys_all, values_all = (
        lax.all_gather(mixed[:, :, features : 2 * features], "ctx", axis=1, tiled=True),
        lax.all_gather(mixed[:, :, 2 * features :], "ctx", axis=1, tiled=True),
    )
    keys_all = keys_all.reshape(seq_count, length, HEADS, HEAD)
    values_all = values_all.reshape(seq_count, length, HEADS, HEAD)
    block_ids = jnp.arange(block_count, dtype=jnp.int32)

    def max_turn(carry, key_index):
        row_top, row_total = carry
        key_start = key_index * key_block
        key_part = lax.dynamic_slice_in_dim(keys_all, key_start, key_block, 1)
        scores = scores_of(query, key_part, key_start, offset, prefix)
        new_top = jnp.maximum(row_top, jnp.max(scores, axis=-1))
        row_total = row_total * jnp.exp(row_top - new_top) + jnp.sum(
            jnp.exp(scores - new_top[..., None]), axis=-1
        )
        return ((new_top, row_total), None)

    stat_shape = (seq_count, HEADS, tok_len)
    (row_top, row_total), unused = lax.scan(
        max_turn,
        (jnp.full(stat_shape, NEG, jnp.float32), jnp.zeros(stat_shape, jnp.float32)),
        block_ids,
    )
    log_total = row_top + jnp.log(row_total)

    def out_turn(summed, key_index):
        key_start = key_index * key_block
        key_part = lax.dynamic_slice_in_dim(keys_all, key_start, key_block, 1)
        value_part = lax.dynamic_slice_in_dim(values_all, key_start, key_block, 1)
        scores = scores_of(query, key_part, key_start, offset, prefix)
        probs = jnp.exp(scores - log_total[..., None]).astype(jnp.bfloat16)
        return (
            summed
            + jnp.einsum("shtk,skhe->sthe", probs, value_part, preferred_element_type=jnp.float32),
            None,
        )

    attended, unused = lax.scan(out_turn, jnp.zeros(query.shape, jnp.float32), block_ids)
    attn_low = attended.astype(jnp.bfloat16).reshape(seq_count * tok_len, features)
    resid = rows_in + (
        jnp.dot(attn_low, w_out, preferred_element_type=jnp.float32) + b_out.astype(jnp.float32)
    )
    factor_ffn, normed2 = norm_rows(resid, gain_ffn.astype(jnp.float32))
    normed_ffn = normed2.astype(jnp.bfloat16)
    pre_act = jnp.dot(normed_ffn, w_up, preferred_element_type=jnp.float32) + b_up.astype(
        jnp.float32
    )
    hidden_low = jnp.square(jax.nn.relu(pre_act)).astype(jnp.bfloat16)
    result = (
        resid
        + jnp.dot(hidden_low, w_down, preferred_element_type=jnp.float32)
        + b_down.astype(jnp.float32)
    )
    saved = (
        rows_in,
        factor_attn,
        normed_low,
        padded,
        query,
        keys_all,
        values_all,
        log_total,
        attended,
        attn_low,
        resid,
        factor_ffn,
        normed_ffn,
        pre_act,
        hidden_low,
    )
    return (saved, result)


def backward_pass(saved, cot_low, prefix, weights, offset):
    (
        rows_in,
        factor_attn,
        normed_low,
        padded,
        query,
        keys_all,
        values_all,
        log_total,
        attended,
        attn_low,
        resid,
        factor_ffn,
        normed_ffn,
        pre_act,
        hidden_low,
    ) = saved
    (
        gain_attn,
        w_query,
        w_key,
        w_value,
        conv_query,
        conv_key,
        conv_value,
        w_out,
        b_out,
        gain_ffn,
        w_up,
        b_up,
        w_down,
        b_down,
    ) = weights
    seq_count, tok_len = (query.shape[0], query.shape[1])
    features = rows_in.shape[1]
    length = keys_all.shape[1]
    key_block = min(512, length)
    block_count = length // key_block
    cot_rows = cot_low.reshape(seq_count * tok_len, features)
    cot_full = cot_rows.astype(jnp.float32)
    grad_bdown = jnp.sum(cot_full, axis=0)
    grad_wdown = outer_sum(hidden_low, cot_rows)
    grad_hidden = back_prod(cot_rows, w_down).astype(jnp.bfloat16)
    grad_pre = (grad_hidden.astype(jnp.float32) * 2.0 * jax.nn.relu(pre_act)).astype(jnp.bfloat16)
    grad_bup = jnp.sum(grad_pre.astype(jnp.float32), axis=0)
    grad_wup = outer_sum(normed_ffn, grad_pre)
    grad_normed = back_prod(grad_pre, w_up)
    resid_part, grad_gffn = norm_back(resid, factor_ffn, gain_ffn.astype(jnp.float32), grad_normed)
    grad_resid = cot_full + resid_part
    grad_branch = grad_resid.astype(jnp.bfloat16)
    grad_bout = jnp.sum(grad_branch.astype(jnp.float32), axis=0)
    grad_wout = outer_sum(attn_low, grad_branch)
    grad_attn = (
        back_prod(grad_branch, w_out).astype(jnp.bfloat16).reshape(seq_count, tok_len, HEADS, HEAD)
    )
    delta = jnp.einsum("sthe,sthe->sht", grad_attn.astype(jnp.float32), attended)
    block_ids = jnp.arange(block_count, dtype=jnp.int32)

    def grad_terms(key_index):
        key_start = key_index * key_block
        key_part = lax.dynamic_slice_in_dim(keys_all, key_start, key_block, 1)
        value_part = lax.dynamic_slice_in_dim(values_all, key_start, key_block, 1)
        scores = scores_of(query, key_part, key_start, offset, prefix)
        probs = jnp.exp(scores - log_total[..., None])
        grad_probs = jnp.einsum(
            "sthe,skhe->shtk", grad_attn, value_part, preferred_element_type=jnp.float32
        )
        grad_scores = (probs * (grad_probs - delta[..., None]) * HEAD ** (-0.5)).astype(
            jnp.bfloat16
        )
        return (key_part, probs, grad_scores)

    def back_turn(summed, key_index):
        key_part, probs, grad_scores = grad_terms(key_index)
        summed = summed + jnp.einsum(
            "shtk,skhe->sthe", grad_scores, key_part, preferred_element_type=jnp.float32
        )
        grad_keys = jnp.einsum(
            "shtk,sthe->skhe", grad_scores, query, preferred_element_type=jnp.float32
        )
        grad_values = jnp.einsum(
            "shtk,sthe->skhe",
            probs.astype(jnp.bfloat16),
            grad_attn,
            preferred_element_type=jnp.float32,
        )
        return (summed, (grad_keys, grad_values))

    grad_query, (grad_keys, grad_values) = lax.scan(
        back_turn, jnp.zeros(query.shape, jnp.float32), block_ids
    )
    grad_keys = jnp.moveaxis(grad_keys, 0, 1).reshape(seq_count, length, features)
    grad_values = jnp.moveaxis(grad_values, 0, 1).reshape(seq_count, length, features)
    own_keys, own_values = (
        lax.psum_scatter(
            grad_keys.astype(jnp.bfloat16), "ctx", scatter_dimension=1, tiled=True
        ).astype(jnp.float32),
        lax.psum_scatter(
            grad_values.astype(jnp.bfloat16), "ctx", scatter_dimension=1, tiled=True
        ).astype(jnp.float32),
    )
    grad_mixed = jnp.concatenate(
        [grad_query.reshape(seq_count, tok_len, features), own_keys, own_values], axis=2
    )
    after = shifted(grad_mixed[:, :2], "ctx", -1)
    extended = jnp.concatenate([grad_mixed, after], axis=1)
    kernel = jnp.concatenate([conv_query, conv_key, conv_value], axis=1).astype(jnp.float32)
    grad_linear = (
        kernel[0] * extended[:, :tok_len]
        + kernel[1] * extended[:, 1 : tok_len + 1]
        + kernel[2] * extended[:, 2:]
    ).astype(jnp.bfloat16)
    grad_kernel = jnp.stack(
        [
            jnp.sum(grad_mixed * padded[:, 2:], axis=(0, 1)),
            jnp.sum(grad_mixed * padded[:, 1 : tok_len + 1], axis=(0, 1)),
            jnp.sum(grad_mixed * padded[:, :tok_len], axis=(0, 1)),
        ]
    )
    grad_lin_rows = grad_linear.reshape(seq_count * tok_len, 3 * features)
    w_joint = jnp.concatenate([w_query, w_key, w_value], axis=1)
    grad_joint = outer_sum(normed_low, grad_lin_rows)
    grad_norm1 = back_prod(grad_lin_rows, w_joint)
    input_part, grad_gattn = norm_back(
        rows_in, factor_attn, gain_attn.astype(jnp.float32), grad_norm1
    )
    input_grad = grad_resid + input_part
    grads = (
        grad_gattn,
        grad_joint[:, :features],
        grad_joint[:, features : 2 * features],
        grad_joint[:, 2 * features :],
        grad_kernel[:, :features],
        grad_kernel[:, features : 2 * features],
        grad_kernel[:, 2 * features :],
        grad_wout,
        grad_bout,
        grad_gffn,
        grad_wup,
        grad_bup,
        grad_wdown,
        grad_bdown,
    )
    return (grads, input_grad)


def general_shards(
    block_input,
    out_grad,
    prefix_len,
    attn_gain,
    q_weight,
    k_weight,
    v_weight,
    conv_q,
    conv_k,
    conv_v,
    out_weight,
    out_bias,
    ffn_gain,
    up_weight,
    up_bias,
    down_weight,
    down_bias,
):
    micro_count = block_input.shape[0]
    local_shape = block_input.shape[1:]
    offset = lax.axis_index("ctx") * block_input.shape[2]
    outputs = []
    input_grads = []
    totals = ()
    for microstep in range(micro_count):
        weights = (
            lax.all_gather(attn_gain, ("dp", "ctx"), axis=0, tiled=True),
            lax.all_gather(q_weight, ("dp", "ctx"), axis=0, tiled=True),
            lax.all_gather(k_weight, ("dp", "ctx"), axis=0, tiled=True),
            lax.all_gather(v_weight, ("dp", "ctx"), axis=0, tiled=True),
            lax.all_gather(conv_q, ("dp", "ctx"), axis=1, tiled=True),
            lax.all_gather(conv_k, ("dp", "ctx"), axis=1, tiled=True),
            lax.all_gather(conv_v, ("dp", "ctx"), axis=1, tiled=True),
            lax.all_gather(out_weight, ("dp", "ctx"), axis=0, tiled=True),
            lax.all_gather(out_bias, ("dp", "ctx"), axis=0, tiled=True),
            lax.all_gather(ffn_gain, ("dp", "ctx"), axis=0, tiled=True),
            lax.all_gather(up_weight, ("dp", "ctx"), axis=0, tiled=True),
            lax.all_gather(up_bias, ("dp", "ctx"), axis=0, tiled=True),
            lax.all_gather(down_weight, ("dp", "ctx"), axis=0, tiled=True),
            lax.all_gather(down_bias, ("dp", "ctx"), axis=0, tiled=True),
        )
        inputs = block_input[microstep].astype(jnp.float32)
        prefix = prefix_len[microstep]
        saved, result = forward_pass(inputs, prefix, weights, offset)
        weights = (
            lax.all_gather(attn_gain, ("dp", "ctx"), axis=0, tiled=True),
            lax.all_gather(q_weight, ("dp", "ctx"), axis=0, tiled=True),
            lax.all_gather(k_weight, ("dp", "ctx"), axis=0, tiled=True),
            lax.all_gather(v_weight, ("dp", "ctx"), axis=0, tiled=True),
            lax.all_gather(conv_q, ("dp", "ctx"), axis=1, tiled=True),
            lax.all_gather(conv_k, ("dp", "ctx"), axis=1, tiled=True),
            lax.all_gather(conv_v, ("dp", "ctx"), axis=1, tiled=True),
            lax.all_gather(out_weight, ("dp", "ctx"), axis=0, tiled=True),
            lax.all_gather(out_bias, ("dp", "ctx"), axis=0, tiled=True),
            lax.all_gather(ffn_gain, ("dp", "ctx"), axis=0, tiled=True),
            lax.all_gather(up_weight, ("dp", "ctx"), axis=0, tiled=True),
            lax.all_gather(up_bias, ("dp", "ctx"), axis=0, tiled=True),
            lax.all_gather(down_weight, ("dp", "ctx"), axis=0, tiled=True),
            lax.all_gather(down_bias, ("dp", "ctx"), axis=0, tiled=True),
        )
        grads, input_grad = backward_pass(saved, out_grad[microstep], prefix, weights, offset)
        totals = (
            grads
            if microstep == 0
            else tuple((earlier + later for earlier, later in zip(totals, grads)))
        )
        outputs.append(result.astype(jnp.bfloat16).reshape(local_shape))
        input_grads.append(input_grad.reshape(local_shape))
    owned = (
        lax.psum_scatter(totals[0], ("dp", "ctx"), scatter_dimension=0, tiled=True),
        lax.psum_scatter(totals[1], ("dp", "ctx"), scatter_dimension=0, tiled=True),
        lax.psum_scatter(totals[2], ("dp", "ctx"), scatter_dimension=0, tiled=True),
        lax.psum_scatter(totals[3], ("dp", "ctx"), scatter_dimension=0, tiled=True),
        lax.psum_scatter(totals[4], ("dp", "ctx"), scatter_dimension=1, tiled=True),
        lax.psum_scatter(totals[5], ("dp", "ctx"), scatter_dimension=1, tiled=True),
        lax.psum_scatter(totals[6], ("dp", "ctx"), scatter_dimension=1, tiled=True),
        lax.psum_scatter(totals[7], ("dp", "ctx"), scatter_dimension=0, tiled=True),
        lax.psum_scatter(totals[8], ("dp", "ctx"), scatter_dimension=0, tiled=True),
        lax.psum_scatter(totals[9], ("dp", "ctx"), scatter_dimension=0, tiled=True),
        lax.psum_scatter(totals[10], ("dp", "ctx"), scatter_dimension=0, tiled=True),
        lax.psum_scatter(totals[11], ("dp", "ctx"), scatter_dimension=0, tiled=True),
        lax.psum_scatter(totals[12], ("dp", "ctx"), scatter_dimension=0, tiled=True),
        lax.psum_scatter(totals[13], ("dp", "ctx"), scatter_dimension=0, tiled=True),
    )
    return (
        jnp.stack(outputs),
        jnp.stack(input_grads),
        owned[0],
        owned[1],
        owned[2],
        owned[3],
        owned[4],
        owned[5],
        owned[6],
        owned[7],
        owned[8],
        owned[9],
        owned[10],
        owned[11],
        owned[12],
        owned[13],
    )


CHIPS = 4
F32 = jnp.float32
BF16 = jnp.bfloat16


def plane_plan(mesh):
    return mesh.shape["ctx"] == 2 * CHIPS and mesh.shape["dp"] == 4


def dot_nn(left, right):
    return jnp.dot(left, right, preferred_element_type=F32)


def dot_nt(left, right):
    return lax.dot_general(left, right, (((1,), (1,)), ((), ())), preferred_element_type=F32)


def dot_tn(left, right):
    return lax.dot_general(left, right, (((0,), (0,)), ((), ())), preferred_element_type=F32)


def call(body, outs, *args, smem=1, hbm=0, scratch=(), name=None, us=0, room=0):
    out_shape = [jax.ShapeDtypeStruct(shape, dtype) for shape, dtype in outs]
    scratch_shapes = [pltpu.VMEM(*spec) if isinstance(spec, tuple) else spec for spec in scratch]
    size = sum(a.size * a.dtype.itemsize for a in args)
    size += sum(int(jnp.dtype(o.dtype).itemsize) * o.size for o in out_shape)
    for spec in scratch:
        if isinstance(spec, tuple):
            size += int(jnp.dtype(spec[1]).itemsize) * functools.reduce(lambda a, b: a * b, spec[0], 1)
    spaces = [pltpu.SMEM] * smem + [pltpu.VMEM] * (len(args) - smem - hbm) + [pltpu.HBM] * hbm
    return pl.pallas_call(
        body,
        out_shape=out_shape,
        compiler_params=pltpu.CompilerParams(vmem_limit_bytes=room or int(size) + (4 << 20)),
        in_specs=[pl.BlockSpec(memory_space=space) for space in spaces],
        out_specs=[pl.BlockSpec(memory_space=pltpu.VMEM)] * len(outs),
        scratch_shapes=scratch_shapes,
        name=name,
        cost_estimate=pl.CostEstimate(flops=1 + us * 10**9, transcendentals=0, bytes_accessed=1),
    )(*args[: len(args) - hbm], *(pltpu.with_memory_space_constraint(a, pltpu.HBM) for a in args[len(args) - hbm :]))


def send(value, bits):
    dp, ctx = lax.axis_size("dp"), lax.axis_size("ctx")
    pairs = [(i, (i // ctx) * ctx + ((i % ctx) ^ bits)) for i in range(dp * ctx)]
    return lax.ppermute(value, ("dp", "ctx"), pairs)


def send_z(value, bits):
    dp, ctx = lax.axis_size("dp"), lax.axis_size("ctx")
    pairs = [(i, ((i // ctx) ^ bits) * ctx + i % ctx) for i in range(dp * ctx)]
    return lax.ppermute(value, ("dp", "ctx"), pairs)


def after(value, *waits):
    return lax.optimization_barrier((value, *waits))[0]


def all_after(values, *waits):
    return list(lax.optimization_barrier((*values, *waits))[: len(values)])


def to_chips(blocks):
    return [blocks[0]] + [send(blocks[j], 2 * j) for j in range(1, CHIPS)]


def stack_k(ids, s0, s1, s2, s3, out):
    for r, ref in enumerate((s0, s1, s2, s3)):
        out[r] = ref[...]


def join_k(ids, mine, other, keep, later, now):
    n = keep.shape[0]
    for r, out in ((0, keep), (2, later), (1, now.at[0]), (3, now.at[1])):
        at = slice(r * n, r * n + n)
        out[...] = (mine[at].astype(F32) + other[at].astype(F32)).astype(BF16)


def pass_on_k(ids, later, got, out):
    out[...] = (later[...].astype(F32) + got[1].astype(F32)).astype(BF16)


def join_cores(ids, keep, away, name):
    size = (keep.shape[0] // 4, *keep.shape[1:])
    return call(
        join_k, [(size, BF16)] * 2 + [((2, *size), BF16)], ids, keep, away, name="join_" + name
    )


def to_all_chips(block):
    half = block.shape[0] // 2
    one, two = send(block, 2), send(block, 4)
    return [block, one, two, send(one[:half], 4), send(two[half:], 2)]


def add_half_k(ids, one, two, low, high, one_out, two_out):
    half = low.shape[0]
    one_out[:half, :] = one[:half, :]
    one_out[half:, :] = (one[half:, :].astype(F32) + high[...].astype(F32)).astype(BF16)
    two_out[half:, :] = two[half:, :]
    two_out[:half, :] = (two[:half, :].astype(F32) + low[...].astype(F32)).astype(BF16)


def to_owners(ids, own, one, two, low, high, *first):
    low, high = all_after([send(low, 2), send(high, 4)], *first)
    one, two = call(add_half_k, [(one.shape, BF16)] * 2, ids, one, two, low, high, name="add_half")
    return own, one, two


ROWS = ((0, 256), (256, 512), (512, 768), (768, 896), (896, 1024))


def place_k(ids, other, mine, out, sem):
    c = ids[2]
    rows = other.shape[2]
    copy = pltpu.make_async_copy(mine.at[c, 0], out.at[pl.ds(pl.multiple_of(c * rows, rows), rows), :], sem)
    copy.start()
    out[pl.ds(pl.multiple_of((1 - c) * rows, rows), rows), :] = other[c, 0]
    copy.wait()


def pack_k(ids, *refs):
    k = ids[1]
    args, (p0, p1, p2, p3), stage, held, sems = refs[:13], refs[13:17], refs[17], refs[18:31], refs[31]
    copies = [pltpu.make_async_copy(ref, to, sems.at[i]) for i, (ref, to) in enumerate(zip(args, held))]
    for copy in copies:
        copy.start()
    for copy in copies:
        copy.wait()
    wq, wk, wv, up, wo, *vectors, bias_u = held
    rows = jnp.concatenate([ref[...].astype(F32).reshape(-1, 24) for ref in vectors], axis=0)
    rows = jnp.concatenate([rows, jnp.zeros((128 - rows.shape[0], 24), F32)], axis=0)
    rows = jnp.concatenate([rows, jnp.zeros((128, 104), F32)], axis=1)
    cols = rows.T[:24, :16]
    bias = bias_u[...].astype(F32).reshape(1, 96)
    bias = jnp.concatenate([bias[:, 24 * i : 24 * i + 24] for i in range(4)] + [jnp.zeros((20, 24), F32)], axis=0)
    tail = jnp.concatenate([cols, bias, jnp.zeros((24, 24), F32)], axis=1).astype(BF16)
    for chip in range(CHIPS):
        lo = 192 * chip
        for part, ref in enumerate((wq, wk, wv)):
            stage[chip, :, 192 * part : 192 * part + 192] = ref[:, lo : lo + 192]
        stage[chip, :, 576:640] = tail
        for plane in range(4):
            at = 640 + 192 * plane
            stage[chip, :, at : at + 192] = up[:, 768 * plane + lo : 768 * plane + lo + 192]
        stage[chip, :, 1408:2176] = wo[...]
    for j, out in enumerate((p0, p1, p2, p3)):
        out[...] = stage[k ^ j]


def split_k(ids, p0, p1, p2, p3, a_out, b_out):
    for j, ref in enumerate((p0, p1, p2, p3)):
        a_out[j] = ref[:, :640]
        b_out[j] = ref[:, 640:1408]
        b_out[CHIPS + j] = ref[:, 1408:2176]


def with_down_k(ids, b, wd, b_out, sems):
    n = b.shape[0]
    copies = [
        pltpu.make_async_copy(wd.at[24 * j : 24 * j + 24, :], b_out.at[n + j], sems.at[j]) for j in range(CHIPS)
    ]
    for copy in copies:
        copy.start()
    b_out[0:n] = b[...]
    for copy in copies:
        copy.wait()


def gather_b_k(ids, mine, other, up_out, wo_out, wd_out):
    z, k, c = ids[0], ids[1], ids[2]
    for core, ref in enumerate((mine, other)):
        for plane in range(4):
            for j in range(CHIPS):
                at = (z ^ plane) * 8 + (k ^ j) * 2 + (c ^ core)
                up_out[at] = ref[plane, j]
                wo_out[at] = ref[plane, CHIPS + j]
                wd_out[((z ^ plane) * 2 + (c ^ core)) * 4 + j] = ref[plane, 8 + j]


def hidden_grad_k(ids, g0, g1, g2, g3, g4, wd, dh, g_all):
    for ref, (lo, hi) in zip((g0, g1, g2, g3, g4), ROWS):
        g_all[lo:hi, :] = ref[...]

    dh[...] = dot_nt(g_all[...], wd[...]).astype(BF16)


def mask_rows(b, prefix, out):
    cols = max(256 * (b + 1), 512)
    row_ids = 256 * b + lax.broadcasted_iota(jnp.int32, (256, cols), 0)
    col_ids = lax.broadcasted_iota(jnp.int32, (256, cols), 1)
    out[:, :cols] = jnp.where((col_ids <= row_ids) | (col_ids < prefix), 0.0, NEG)
    return cols


def attend_k(
    ids, pre, *refs,
):
    n_x = len(refs) - 21
    pieces, xs, refs = refs[:2], refs[2 : 2 + n_x], refs[2 + n_x :]
    w_out, bias_out, a_out, lin, q_out, k_out, v_out, o0, o1, o2, o3, att, lse, small_out, kern_out = refs[:15]
    w_scr, stage, mask, mixed = refs[15:]
    z, k, c = ids[0], ids[1], ids[2]
    prefix = pre[c, 0]
    for core in range(2):
        for plane in range(4):
            for j in range(CHIPS):
                w_scr[(z ^ plane) * 8 + (k ^ j) * 2 + (c ^ core)] = pieces[core][plane, j].astype(F32)
    bias_out[...] = jnp.zeros_like(bias_out)
    for plane in range(4):
        for core in range(2):
            piece = w_scr[plane * 8 + k * 2 + core, :, 512:640]
            for part in range(4):
                at = 96 * (2 * plane + core) + 24 * part
                bias_out[0:1, at : at + 24] = piece[part : part + 1, 80:104]
    small = w_scr[:, :, 512:640].reshape(768, 128).T[64:80]
    w_out[...] = w_scr[:, :, 0:576].reshape(768, 576).astype(BF16)
    small_out[...] = small
    gain = small[0:1]
    own = jnp.zeros((9, 192), F32)
    for chip in range(CHIPS):
        own = jnp.where(k == chip, small[1:10, 192 * chip : 192 * chip + 192], own)
    kern = jnp.concatenate([own[0:3], own[3:6], own[6:9]], axis=1)
    kern_out[...] = kern
    lin[0:8, :] = jnp.zeros((8, lin.shape[1]), F32)
    for ref, (lo, hi) in zip(xs, ROWS if n_x == 5 else ROWS[:3] + ((768, 1024),)):
        at = pl.multiple_of((k ^ (lo // 256)) * 256 + lo % 256, 128)
        x = ref[...].astype(F32)
        factor = lax.rsqrt(jnp.mean(x * x, axis=-1, keepdims=True) + EPS)
        a_out[pl.ds(at, hi - lo), :] = (x * factor * gain).astype(BF16)

    for b in range(4):
        at = 256 * b
        lin[at + 8 : at + 264, :] = dot_nn(a_out[at : at + 256, :], w_out[...])
    for b in range(4):
        t = 256 * b
        mixed[...] = (
            kern[0:1] * lin[8 + t : 264 + t, :]
            + kern[1:2] * lin[7 + t : 263 + t, :]
            + kern[2:3] * lin[6 + t : 262 + t, :]
        ).astype(BF16)
        for h in range(3):
            lo = 64 * h
            q_out[h, t : t + 256, :] = mixed[:, lo : lo + 64] * BF16(HEAD ** (-0.5))
            k_out[h, t : t + 256, :] = mixed[:, 192 + lo : 256 + lo]
            v_out[h, t : t + 256, :] = mixed[:, 384 + lo : 448 + lo]
    for b in range(4):
        t = 256 * b
        cols = mask_rows(b, prefix, mask)

        for h in range(3):
            scores = dot_nt(q_out[h, t : t + 256, :], k_out[h, 0:cols, :]) + mask[:, :cols]
            top = jnp.max(scores, axis=-1, keepdims=True)
            weight = jnp.exp(scores - top)
            total = jnp.sum(weight, axis=-1, keepdims=True)
            att[h, t : t + 256, :] = dot_nn(weight.astype(BF16), v_out[h, 0:cols, :]) * (1.0 / total)
            lse[h, t : t + 256, :] = top + jnp.log(total)
        stage[b] = jnp.concatenate([att[h, t : t + 256, :] for h in range(3)], axis=1).astype(BF16)
    for j, out in enumerate((o0, o1, o2, o3)):
        out[...] = stage[k ^ j]


def resid_k(ids, t0, t1, t2, t3, wo, xw, small, x1_out, a2_out):
    k = ids[1]
    total = xw[...].astype(F32) + small[10:11]
    for j, ref in enumerate((t0, t1, t2, t3)):
        at = pl.multiple_of((k ^ j) * 192, 192)
        total = total + dot_nn(ref[...], wo[pl.ds(at, 192), :])
    x1_out[...] = total
    factor = lax.rsqrt(jnp.mean(total * total, axis=-1, keepdims=True) + EPS)
    a2_out[...] = (total * factor * small[11:12]).astype(BF16)


def ffn_k(ids, *refs):
    n_a = len(refs) - 12
    blocks, refs = refs[:n_a], refs[n_a:]
    dh, up, bias, hsq, du, a_all, p0, p1, p2, p3, p4, stage = refs
    for ref, (lo, hi) in zip(blocks, ROWS if n_a == 5 else ROWS[:3] + ((768, 1024),)):
        a_all[lo:hi, :] = ref[...]

    act = jax.nn.relu(dot_nn(a_all[...], up[...]) + bias[...])
    hsq[...] = (act * act).astype(BF16)
    du[...] = (dh[...].astype(F32) * 2.0 * act).astype(BF16)
    stage[...] = dot_nt(du[...], up[...]).astype(BF16)
    for ref, (lo, hi) in zip((p0, p1, p2, p3, p4), ROWS):
        ref[...] = stage[lo:hi, :]


def ffn_out_k(ids, hsq, wd, p0, p1, p2, p3):
    for j, out in enumerate((p0, p1, p2, p3)):
        out[...] = dot_nn(hsq[256 * j : 256 * j + 256, :], wd[...]).astype(BF16)


def ffn_grads_k(ids, a_all, g_all, hsq, du, keep, away, bias_out, stage):
    z, k, c = ids[0], ids[1], ids[2]
    bias_out[...] = jnp.sum(du[...].astype(F32), axis=0, keepdims=True)
    up_grad = dot_tn(a_all[...], du[...])
    for plane in range(4):
        for core in range(2):
            to, at = c ^ core, (z ^ plane) * 8
            for chip in range(CHIPS):
                row = 24 * (plane * 8 + chip * 2 + core)
                stage[to, at + (k ^ chip)] = up_grad[row : row + 24].astype(BF16)
    down_grad = dot_tn(hsq[...], g_all[...])
    for plane in range(4):
        for core in range(2):
            to, at = c ^ core, (z ^ plane) * 8
            for chip in range(CHIPS):
                row = 96 * (plane * 2 + core) + 24 * chip
                stage[to, at + 4 + chip] = down_grad[row : row + 24].astype(BF16)
    keep[...] = stage[0]
    away[...] = stage[1]


def sum_planes_k(ids, *refs):
    f, o, r, (d_out, *outs) = refs[0:3], refs[3:6], refs[6:9], refs[9:]

    def total(parts, at):
        return parts[0][at].astype(F32) + parts[1][0, at].astype(F32) + parts[2][at].astype(F32)

    for j, out in enumerate(outs):
        out[:, 0:640] = total(r, j).astype(BF16)
        out[:, 640:1408] = total(f, j).astype(BF16)
        out[:, 1408:2176] = total(o, j).astype(BF16)
        d_out[24 * j : 24 * j + 24, :] = total(f, CHIPS + j)


def mid_grad_k(
    ids, p0, p1, p2, x1, gw, small, wo, dx_out, dz_out, bias_out, o0, o1, o2, o3
):
    k = ids[1]
    da2 = p0[...].astype(F32) + p1[...].astype(F32) + p2[...].astype(F32)
    val = x1[...]
    factor = lax.rsqrt(jnp.mean(val * val, axis=-1, keepdims=True) + EPS)
    weighted = da2 * small[11:12]
    inner = jnp.mean(weighted * val, axis=-1, keepdims=True)
    dx = gw[...].astype(F32) + factor * weighted - val * (factor * factor * factor * inner)
    dx_out[...] = dx
    low = dx.astype(BF16)
    dz_out[...] = low
    bias_out[...] = jnp.sum(low.astype(F32), axis=0, keepdims=True)
    for j, out in enumerate((o0, o1, o2, o3)):
        at = pl.multiple_of((k ^ j) * 192, 192)
        out[...] = dot_nt(low, wo[pl.ds(at, 192), :]).astype(BF16)


def out_grads_k(ids, t0, t1, t2, t3, dz, keep, away, stage):
    z, k, c = ids[0], ids[1], ids[2]
    for j, ref in enumerate((t0, t1, t2, t3)):
        part = dot_tn(ref[...], dz[...])
        at = ((k ^ j) ^ z) * 4
        for chip in range(CHIPS):
            for core in range(2):
                row = 24 * (2 * chip + core)
                stage[c ^ core, at + (k ^ chip)] = part[row : row + 24].astype(BF16)
    keep[...] = stage[0]
    away[...] = stage[1]


def attend_grad_k(
    ids, pre, d0, d1, d2, d3, q_in, k_in, v_in, att, lse, lin, kern, w,
    dlin_out, conv_out, p0, p1, p2, p3, p4, do_scr, dm, mask, dq, dk, dv, stage,
):
    k, c = ids[1], ids[2]
    prefix = pre[c, 0]
    for j, ref in enumerate((d0, d1, d2, d3)):
        for h in range(3):
            do_scr[h, pl.ds(pl.multiple_of((k ^ j) * 256, 256), 256), :] = ref[:, 64 * h : 64 * h + 64]
    dm[1024:1032, :] = jnp.zeros((8, 576), F32)
    for b in (3, 2, 1, 0):
        t = 256 * b
        cols = mask_rows(b, prefix, mask)

        for h in range(3):
            q_rows, do_rows = q_in[h, t : t + 256, :], do_scr[h, t : t + 256, :]
            scores = dot_nt(q_rows, k_in[h, 0:cols, :]) + mask[:, :cols]
            probs = jnp.exp(scores - lse[h, t : t + 256, :])
            delta = jnp.sum(do_rows.astype(F32) * att[h, t : t + 256, :], axis=-1, keepdims=True)
            dprobs = dot_nt(do_rows, v_in[h, 0:cols, :])
            dscores = (probs * (dprobs - delta)).astype(BF16)
            dq[h, t : t + 256, :] = dot_nn(dscores, k_in[h, 0:cols, :]) * HEAD ** (-0.5)
            dk_part = dot_tn(q_rows, dscores)
            dv_part = dot_tn(do_rows, probs.astype(BF16))
            if b == 3:
                dk[h] = dk_part
                dv[h] = dv_part
            else:
                dk[h, :, 0:cols] = dk[h, :, 0:cols] + dk_part
                dv[h, :, 0:cols] = dv[h, :, 0:cols] + dv_part
    for h in range(3):
        dm[0:1024, 64 * h : 64 * h + 64] = dq[h]
        dm[0:1024, 192 + 64 * h : 256 + 64 * h] = dk[h].T
        dm[0:1024, 384 + 64 * h : 448 + 64 * h] = dv[h].T
    taps = kern[...]
    sums = [jnp.zeros((1, 576), F32) for _ in range(3)]
    for b in range(4):
        t = 256 * b
        here = dm[t : t + 256, :]
        dlin_out[t : t + 256, :] = (
            taps[0:1] * here + taps[1:2] * dm[t + 1 : t + 257, :] + taps[2:3] * dm[t + 2 : t + 258, :]
        ).astype(BF16)
        for back in range(3):
            sums[back] = sums[back] + jnp.sum(
                here * lin[8 - back + t : 264 - back + t, :], axis=0, keepdims=True
            )
    conv_out[...] = jnp.concatenate(sums, axis=0)

    stage[...] = dot_nt(dlin_out[...], w[...]).astype(BF16)
    for ref, (lo, hi) in zip((p0, p1, p2, p3, p4), ROWS):
        at = pl.multiple_of((k ^ (lo // 256)) * 256 + lo % 256, 128)
        ref[...] = stage[pl.ds(at, hi - lo), :]


def proj_grads_k(ids, a1, dlin, conv, up_bias, out_bias, g, keep, away, stage):
    z, k, c = ids[0], ids[1], ids[2]
    grad = dot_tn(a1[...], dlin[...])
    conv_rows = jnp.concatenate([conv[:, 0:192], conv[:, 192:384], conv[:, 384:576]], axis=0)
    conv_all = jnp.concatenate(
        [jnp.where(k == chip, conv_rows, 0.0) for chip in range(CHIPS)], axis=1
    )
    down_bias = jnp.sum(g[...].astype(F32), axis=0, keepdims=True)
    rows = jnp.concatenate(
        [conv_all, out_bias[...], down_bias, jnp.zeros((117, 768), F32)], axis=0
    )
    cols = rows.T
    for plane in range(4):
        for chip in range(CHIPS):
            for core in range(2):
                row = 24 * (plane * 8 + chip * 2 + core)
                to, at = c ^ core, (z ^ plane) * 4 + (k ^ chip)
                stage[to, at, :, 0:576] = grad[row : row + 24]
                stage[to, at, :, 576:640] = cols[row : row + 24, 0:64]
    for plane in range(4):
        for core in range(2):
            for part in range(4):
                lo = 96 * (2 * plane + core) + 24 * part
                stage[c ^ core, (z ^ plane) * 4, part : part + 1, 592:616] = up_bias[0:1, lo : lo + 24]
    keep[...] = stage[0].astype(BF16)
    away[...] = stage[1].astype(BF16)


def halves_k(ids, total_fn, keep, away):
    c = ids[2]
    keep[...] = total_fn(pl.ds(pl.multiple_of(c * 128, 128), 128)).astype(keep.dtype)
    away[...] = total_fn(pl.ds(pl.multiple_of((1 - c) * 128, 128), 128)).astype(away.dtype)


def output_k(ids, p0, p1, p2, p3, x1, small, keep, away):
    def rows_of(at):
        total = p0[at, :].astype(F32) + p1[at, :].astype(F32) + p2[at, :].astype(F32)
        return x1[at, :] + (total + p3[at, :].astype(F32)) + small[12:13]

    halves_k(ids, rows_of, keep, away)


def input_grad_k(ids, p0, p1, p2, xw, dx, small, keep, away):
    def rows_of(at):
        da1 = p0[at, :].astype(F32) + p1[at, :].astype(F32) + p2[at, :].astype(F32)
        val = xw[at, :].astype(F32)
        factor = lax.rsqrt(jnp.mean(val * val, axis=-1, keepdims=True) + EPS)
        weighted = da1 * small[0:1]
        inner = jnp.mean(weighted * val, axis=-1, keepdims=True)
        return dx[at, :] + factor * weighted - val * (factor * factor * factor * inner)

    halves_k(ids, rows_of, keep, away)


def deliver_k(ids, out_keep, out_recv, in_keep, in_recv, out_ref, in_ref):
    c = ids[2]
    out_ref[c, 0] = out_keep[...]
    out_ref[1 - c, 0] = out_recv[...]
    in_ref[c, 0] = in_keep[...]
    in_ref[1 - c, 0] = in_recv[...]


def owned_k(
    ids, s0, s1, s2, s3, wq, wk, wv, up, gain_a, gain_f,
    gq, gk, gv, cq, ck, cv, go, gu, ga, gf, bo, bd, bu, stage_r, stage_u,
):
    k = ids[1]
    extra = jnp.zeros((24, 128), F32)
    out_sum = jnp.zeros((24, 768), F32)
    for j, ref in enumerate((s0, s1, s2, s3)):
        stage_r[k ^ j] = ref[:, 0:640].astype(F32)
        stage_u[k ^ j] = ref[:, 640:1408].astype(F32)
        out_sum = out_sum + ref[:, 1408:2176].astype(F32)
        extra = extra + ref[:, 512:640].astype(F32)
    go[...] = out_sum
    for chip in range(CHIPS):
        lo = 192 * chip
        for part, ref in enumerate((gq, gk, gv)):
            ref[:, lo : lo + 192] = stage_r[chip, :, 192 * part : 192 * part + 192]
        for plane in range(4):
            at = 768 * plane + lo
            gu[:, at : at + 192] = stage_u[chip, :, 192 * plane : 192 * plane + 192]
    attn = jnp.sum(
        gq[...] * wq[...].astype(F32) + gk[...] * wk[...].astype(F32) + gv[...] * wv[...].astype(F32),
        axis=-1, keepdims=True,
    )
    ffn = jnp.sum(gu[...] * up[...].astype(F32), axis=-1, keepdims=True)
    cols = jnp.concatenate([extra[:, 64:75], attn, ffn, jnp.zeros((24, 115), F32)], axis=1)
    cols = jnp.concatenate([cols, jnp.zeros((104, 128), F32)], axis=0)
    rows = cols.T[:16, :24]
    for at, ref in ((0, cq), (3, ck), (6, cv)):
        ref[...] = rows[at : at + 3]
    bo[...] = rows[9]
    bd[...] = rows[10]
    ga[...] = rows[11] / gain_a[...].astype(F32)
    gf[...] = rows[12] / gain_f[...].astype(F32)
    bu[...] = jnp.concatenate([extra[i : i + 1, 80:104] for i in range(4)], axis=1).reshape(96)


def plane_shards(block_input, out_grad, prefix_len, attn_gain, q_weight, k_weight, v_weight, conv_q, conv_k, conv_v, out_weight, out_bias, ffn_gain, up_weight, up_bias, down_weight, down_bias):
    z, place = (lax.axis_index('dp'), lax.axis_index('ctx'))
    ids = jnp.stack([z, place // 2, place % 2]).astype(jnp.int32)
    block, half = (((256, 768), BF16), ((128, 768), BF16))
    blocks = [block] * 3 + [half] * 2
    tall, heads = (((1024, 768), BF16), (3, 1024, 64))
    rows = (128, 768)
    sem = pltpu.SemaphoreType.DMA
    x_peer = send(block_input, 1)
    weights = (q_weight, k_weight, v_weight, up_weight, out_weight, attn_gain, conv_q, conv_k, conv_v, out_bias, ffn_gain, down_bias, up_bias)
    packs = call(pack_k, [((24, 2176), BF16)] * 4, ids, *weights, hbm=13, scratch=[((4, 24, 2176), BF16)] + [(w.shape, BF16) for w in weights] + [sem((13,))], name='pack')
    packs = to_chips(packs)
    x_peer = after(x_peer, *packs[1:2])
    xw, = call(place_k, [block], ids, x_peer, block_input, hbm=1, scratch=[sem(())], name='place_x')
    x_one, x_two = (send(xw, 2), send(xw, 4))
    a_own, b_own = call(split_k, [((4, 24, 640), BF16), ((8, 24, 768), BF16)], ids, *packs, name='split')
    a_two, a_one = (send_z(a_own, 2), send_z(a_own, 1))
    a_three = send_z(a_own, 3)
    x_low, x_high = (send(part, bits) for part, bits in zip(all_after([x_one[:128], x_two[128:]], a_two), (4, 2)))
    xs = [xw, x_one, x_two, x_low, x_high]
    bdep = ()
    b_own, = call(with_down_k, [((12, 24, 768), BF16)], ids, after(b_own, *bdep), down_weight, hbm=1, scratch=[sem((4,))], name='with_down')
    wd_dep = b_own
    g_peer = send(after(out_grad, *packs[1:]), 1)
    gw, = call(place_k, [block], ids, g_peer, out_grad, hbm=1, scratch=[sem(())], name='place_g')
    a_last = after(a_three, wd_dep)
    a_all, = call(stack_k, [((4, 4, 24, 640), BF16)], ids, a_own, a_one, a_two, a_last, name='stack_a')
    a_peer = send(a_all, 1)
    b_own = after(b_own, a_three)
    b_one, b_two = (send_z(b_own, 1), send_z(b_own, 2))
    gsrc = after(gw, *xs[1:3])
    g_one, g_two = (send(gsrc, 2), send(gsrc, 4))
    w_a, up_bias_row, a1, lin, q, k, v, t0, t1, t2, t3, att, lse, small, kern = call(attend_k, [((768, 576), BF16), ((1, 768), F32), tall, ((1032, 576), F32)] + [(heads, BF16)] * 3 + [((256, 192), BF16)] * 4 + [(heads, F32), ((3, 1024, 1), F32), ((16, 768), F32), ((3, 576), F32)], ids, prefix_len, after(a_all, gw), a_peer, *xs, smem=2, name='attend', scratch=[((32, 24, 640), F32), ((4, 256, 192), BF16), ((256, 1024), F32), ((256, 576), BF16)])
    atts = [t0, send(t1, 2), send(t2, 4)]
    atts.append(send(after(t3, *atts[1:2]), 6))
    g_one, g_two = all_after([g_one, g_two], t1)
    g_low, g_high = (send(part, bits) for part, bits in zip([g_one[:128], g_two[128:]], (4, 2)))
    sdep = [*atts[1:3], *(g_low, g_high)]
    b_one, b_two = all_after([b_one, b_two], t1)
    b_three = send_z(b_two, 1)
    b_all, = call(stack_k, [((4, 12, 24, 768), BF16)], ids, b_own, *all_after([b_one, b_two, b_three], *sdep), name='stack_b')
    w_up, w_o, w_d = [w.reshape(768, 768) for w in call(gather_b_k, [((32, 24, 768), BF16)] * 3, ids, b_all, send(b_all, 1), name='gather_b')]
    x1, a2 = call(resid_k, [((256, 768), F32), block], ids, *atts, w_o, xw, small, name='resid')
    a2s = to_all_chips(a2)
    dh, g_all = call(hidden_grad_k, [tall] * 2, ids, gw, g_one, g_two, g_low, g_high, w_d, name='hidden_grad')
    hsq, du, a2_all, *da2 = call(ffn_k, [tall] * 3 + blocks, ids, *a2s, dh, w_up, up_bias_row, scratch=[tall], name='ffn')
    da2_parts = da2
    f_keep, f_away, up_bias_grad = call(ffn_grads_k, [((32, 24, 768), BF16)] * 2 + [((1, 768), F32)], ids, a2_all, g_all, hsq, du, scratch=[((2, 32, 24, 768), BF16)], name='ffn_grads', us=1000)
    d_first = []
    d_first.append(up_bias_grad)
    da2, da2_one, da2_two = to_owners(ids, *da2_parts, *d_first)
    da2 = [da2, send(da2_one, 2), send(da2_two, 4)]
    mid_first = []
    outs = list(call(ffn_out_k, [block] * 4, ids, hsq, after(w_d, da2_one), name='ffn_out'))
    mid_first.append(outs[0])
    f_peer = send(after(f_away, da2_one), 1)
    f_keep, f_later, f_now = join_cores(ids, f_keep, f_peer, 'f')
    f_now = send_z(f_now, 1)
    mid_first.append(f_keep)
    dx, dz, out_bias_grad, *datt = call(mid_grad_k, [((256, 768), F32), block, ((1, 768), F32)] + [((256, 192), BF16)] * 4, ids, *da2, x1, after(gw, *mid_first), small, w_o, name='mid_grad')
    datt = to_chips(datt)
    ag_first = []
    o_keep, o_away = call(out_grads_k, [((16, 24, 768), BF16)] * 2, ids, *atts, dz, scratch=[((2, 16, 24, 768), BF16)], name='out_grads')
    ag_first.append(o_keep)
    pj_first = []
    f_now = after(f_now, *datt[1:])
    f_later, = call(pass_on_k, [(f_later.shape, BF16)], ids, f_later, f_now, name='pass_f')
    f_sent = send_z(f_later, 2)
    ag_first.append(f_later)
    pj_first.append(f_sent)
    outs[1:] = all_after(outs[1:], *datt[1:])
    outs[1], outs[2] = (send(outs[1], 2), send(outs[2], 4))
    pj_first += outs[1:3]
    dlin, conv_grad, *da1 = call(attend_grad_k, [((1024, 576), BF16), ((3, 576), F32)] + blocks, ids, prefix_len, *datt, after(q, *ag_first), k, v, att, lse, lin, kern, w_a, smem=2, name='attend_grad', scratch=[(heads, BF16), ((1032, 576), F32), ((256, 1024), F32), (heads, F32)] + [((3, 64, 1024), F32)] * 2 + [tall])
    o_peer = send(after(o_away, dlin), 1)
    r_keep, r_away = call(proj_grads_k, [((16, 24, 640), BF16)] * 2, ids, after(a1, *pj_first), dlin, conv_grad, up_bias_grad, out_bias_grad, gw, scratch=[((2, 16, 24, 640), F32)], name='proj_grads')
    r_peer = send(r_away, 1)
    r_keep, r_later, r_now = join_cores(ids, r_keep, r_peer, 'r')
    r_now = send_z(r_now, 1)
    o_keep, o_later, o_now = join_cores(ids, o_keep, o_peer, 'o')
    o_now = send_z(o_now, 1)
    o_now = after(o_now, r_keep)
    o_later, = call(pass_on_k, [(o_later.shape, BF16)], ids, o_later, o_now, name='pass_o')
    o_sent = send_z(o_later, 2)
    da1, da1_one, da1_two = to_owners(ids, *da1)
    r_later, = call(pass_on_k, [(r_later.shape, BF16)], ids, r_later, r_now, name='pass_r')
    da1 = [da1, send(da1_one, 2), send(da1_two, 4)]
    r_sent = send_z(r_later, 2)
    outs[3] = send(after(outs[3], r_keep), 6)
    out_keep, out_away = call(output_k, [(rows, BF16)] * 2, ids, *outs, after(x1, r_later), small, name='output')
    out_recv = send(out_away, 1)
    in_keep, in_away = call(input_grad_k, [(rows, F32)] * 2, ids, *da1, xw, dx, small, name='input_grad')
    in_recv = send(in_away, 1)
    o_parts = [o_keep, o_now, o_sent]
    f_parts = [f_keep, f_now, f_sent]
    r_parts = [r_keep, r_now, r_sent]
    down_grad, *sums = call(sum_planes_k, [((96, 768), F32)] + [((24, 2176), BF16)] * 4, ids, *f_parts, *o_parts, *r_parts, name='sum_planes')
    sums = to_chips(sums)
    block_output, input_grad = call(deliver_k, [((2, 1, 128, 768), BF16), ((2, 1, 128, 768), F32)], ids, out_keep, out_recv, in_keep, in_recv, name='deliver', us=100)
    vec = ((24,), F32)
    gq, gk, gv, cq, ck, cv, go, gu, ga, gf, bo, bd, bu = call(owned_k, [((24, 768), F32)] * 3 + [((3, 24), F32)] * 3 + [((24, 768), F32), ((24, 3072), F32)] + [vec] * 4 + [((96,), F32)], ids, sums[0], *sums[1:], q_weight, k_weight, v_weight, up_weight, attn_gain, ffn_gain, scratch=[((4, 24, 640), F32), ((4, 24, 768), F32)], name='owned', us=100)
    return (block_output, input_grad, ga, gq, gk, gv, cq, ck, cv, go, bo, gf, gu, bu, down_grad, bd)


def solution(mesh):
    plan = plane_shards if plane_plan(mesh) else general_shards
    in_specs = (
        P(None, "dp", "ctx", None),
        P(None, "dp", "ctx", None),
        P(None, "dp"),
        P(("dp", "ctx")),
        P(("dp", "ctx"), None),
        P(("dp", "ctx"), None),
        P(("dp", "ctx"), None),
        P(None, ("dp", "ctx")),
        P(None, ("dp", "ctx")),
        P(None, ("dp", "ctx")),
        P(("dp", "ctx"), None),
        P(("dp", "ctx")),
        P(("dp", "ctx")),
        P(("dp", "ctx"), None),
        P(("dp", "ctx")),
        P(("dp", "ctx"), None),
        P(("dp", "ctx")),
    )
    out_specs = (
        P(None, "dp", "ctx", None),
        P(None, "dp", "ctx", None),
        P(("dp", "ctx")),
        P(("dp", "ctx"), None),
        P(("dp", "ctx"), None),
        P(("dp", "ctx"), None),
        P(None, ("dp", "ctx")),
        P(None, ("dp", "ctx")),
        P(None, ("dp", "ctx")),
        P(("dp", "ctx"), None),
        P(("dp", "ctx")),
        P(("dp", "ctx")),
        P(("dp", "ctx"), None),
        P(("dp", "ctx")),
        P(("dp", "ctx"), None),
        P(("dp", "ctx")),
    )
    return jax.shard_map(plan, mesh=mesh, in_specs=in_specs, out_specs=out_specs, check_vma=False)
```
